32 devices in a mesh: slab: 2 (over y), sec: 8 (over z, x), tile: 2 (over core).
Axes of the slice: x: 2, y: 2, z: 4, core: 2. Of those that a mesh axis runs over, the one named last changes fastest.
Arguments:
- image: bfloat16 [16, 128, 4096], P(('slab', 'sec'), 'tile'), parts along dimension 0, may hold values from -6 to 6
- keyframe: int32 [16], P(('slab', 'sec')), parts along dimension 0, may hold values from 0 to 7, as said below
- offsets: int32 [16, 64], P(('slab', 'sec')), parts along dimension 0, may hold values from -16 to 16
Outputs:
- warped: bfloat16 [16, 128, 4096], P(('slab', 'sec'), 'tile'), parts along dimension 0
- field: float32 [16, 2, 2, 64], P(('slab', 'sec'), None, 'tile'), parts along dimension 0
- pyramid: float32 [16, 16, 512], P(('slab', 'sec'), 'tile'), parts along dimension 0
The draws below stay inside these ranges and needn't reach their ends.
There are 2 independent parts, one for each index of `slab`. The reference program is written for one: setup_inputs(seed, part) draws one part's arguments, and reference() takes and returns one part's arrays. A program takes and returns all parts, laid end to end along the dimension named above; each array names one. Nothing has to cross between parts.
Inputs may be any that keep to these rules, and one draw needn't show every extreme that they name: Sections 0, 3 and 7 are keyframes and section 4 is not; keyframe[s] is the largest keyframe index at or before s, and a keyframe is its own keyframe.
All inputs are finite; a program needn't handle non-finite values.
Results may differ from the reference program's by a relative error of at most 0.0033.
Values may be sent and summed in bfloat16 or wider, within the bound.
A program may use at most 64 MiB of HBM per device.

```python
import jax
import jax.numpy as jnp
from jax import lax

W = 4096
PATCH = 64
KCOEF = 8
OFFMAX = 16
WIN = 8
SECTIONS = 8
ROWS = 128


def draw_keyframe(key, part):
    marks = jax.random.randint(jax.random.fold_in(key, 71), (SECTIONS,), 0, 2) == 0
    index = jnp.arange(SECTIONS, dtype=jnp.int32)
    middle = SECTIONS // 2
    marks = marks | (index == 0) | (index == SECTIONS - 1) | (index == middle - 1)
    marks = marks & (index != middle)
    return lax.cummax(jnp.where(marks, index, 0), axis=0).astype(jnp.int32)


def plant(array, stream_key, smallest, largest):
    index_at = [jax.random.randint(jax.random.fold_in(stream_key, axis), (), 0, length) for axis, length in enumerate(array.shape)]
    longest = array.shape.index(max(array.shape))
    neighbour = index_at[:longest] + [(index_at[longest] + 1) % array.shape[longest]] + index_at[longest + 1:]
    return array.at[tuple(index_at)].set(smallest).at[tuple(neighbour)].set(largest)


def block_levels(stream_key, shape, cuts, low, high):
    factor_of = 1.0
    for axis_at, shards_of in cuts:
        steps = jax.random.uniform(jax.random.fold_in(jax.random.fold_in(stream_key, 6), axis_at), (shards_of,), jnp.float32, low / len(cuts), high / len(cuts))
        factor_of = factor_of * jnp.repeat(jnp.exp(steps), shape[axis_at] // shards_of).reshape((-1,) + (1,) * (len(shape) - 1 - axis_at))
    return factor_of


def normal_values(key, dims, deviation, bound, cuts=(), held_as=jnp.bfloat16):
    values = deviation * jax.random.normal(key, dims, jnp.float32)
    if cuts:
        values = values * block_levels(key, dims, cuts, -0.22, 0.18)
    return jnp.clip(values, -bound, bound).astype(held_as)


def setup_inputs(seed: int = 0, part: int = 0) -> dict:
    streams_of = jax.random.split(jax.random.key(seed), 4)
    own_keys = jax.random.split(jax.random.fold_in(streams_of[3], part), 4)
    image = normal_values(own_keys[0], (SECTIONS, ROWS, W), 1.0, 6.0, ((0, 8), (1, 2)))
    keyframe = draw_keyframe(jax.random.fold_in(jax.random.fold_in(streams_of[3], part), 71), part)
    offsets = plant(jax.random.randint(own_keys[2], (SECTIONS, W // PATCH), 0 - OFFMAX, OFFMAX + 1), jax.random.fold_in(own_keys[2], 1), 0 - OFFMAX, OFFMAX).astype(jnp.int32)
    return {"image": image, "keyframe": keyframe, "offsets": offsets}


HIGH = lax.Precision.HIGHEST
REG = 4.0

def cosine_table():
    index = jnp.arange(PATCH, dtype=jnp.float32)
    order = jnp.arange(KCOEF, dtype=jnp.float32)
    table = jnp.sqrt(2.0 / PATCH) * jnp.cos(jnp.pi * (index[None, :] + 0.5) * order[:, None] / PATCH)
    scale = jnp.where(order == 0, jnp.sqrt(0.5), 1.0)
    return (table * scale[:, None]).astype(jnp.float32)

def describe(field, table):
    rows, cols = field.shape
    first = jnp.einsum('rtj,bj->rtb', field.reshape(rows, cols // PATCH, PATCH), table, precision=HIGH)
    first = first.reshape(rows // PATCH, PATCH, cols // PATCH * KCOEF)
    second = jnp.einsum('pic,ai->pac', first, table, precision=HIGH)
    return second.reshape(rows // PATCH * KCOEF, cols // PATCH * KCOEF)

def patch_sums(values):
    rows, cols = values.shape
    return values.reshape(rows // KCOEF, KCOEF, cols // KCOEF, KCOEF).sum(axis=(1, 3))

def displacement(desc, d_col, d_row, refer):
    diff = refer.astype(jnp.float32) - desc.astype(jnp.float32)
    gxx = patch_sums(d_col * d_col) + REG
    gxy = patch_sums(d_col * d_row)
    gyy = patch_sums(d_row * d_row) + REG
    b_col = patch_sums(d_col * diff)
    b_row = patch_sums(d_row * diff)
    det = gxx * gyy - gxy * gxy
    return ((gyy * b_col - gxy * b_row) / det, (gxx * b_row - gxy * b_col) / det)

def taps(shift):
    return (-shift * (shift - 1.0) * (shift - 2.0) / 6.0, (shift + 1.0) * (shift - 1.0) * (shift - 2.0) / 2.0, -(shift + 1.0) * shift * (shift - 2.0) / 2.0, (shift + 1.0) * shift * (shift - 1.0) / 6.0)

def warp(extended, u_col, u_row, offs):
    rows = extended.shape[0] - 4
    cols = extended.shape[1]
    prow, pcol = (rows // PATCH, cols // PATCH)
    vert = jnp.zeros((prow, PATCH, pcol, PATCH), jnp.float32)
    for k, weight in enumerate(taps(u_row)):
        part = extended[1 + k:1 + k + rows].reshape(prow, PATCH, pcol, PATCH)
        vert = vert + weight[:, None, :, None] * part
    padded = jnp.pad(vert, ((0, 0), (0, 0), (1, 1), (0, 0)))
    window = jnp.concatenate([padded[:, :, 0:pcol], padded[:, :, 1:pcol + 1], padded[:, :, 2:pcol + 2]], axis=-1)
    widx = jnp.arange(3 * PATCH, dtype=jnp.int32)[None, None, :, None]
    jidx = jnp.arange(PATCH, dtype=jnp.int32)[None, None, None, :]
    base = jidx + PATCH + offs.astype(jnp.int32)[None, :, None, None]
    matrix = jnp.zeros((prow, pcol, 3 * PATCH, PATCH), jnp.float32)
    for k, weight in enumerate(taps(u_col)):
        matrix = matrix + weight[:, :, None, None] * (widx == base + (k - 1)).astype(jnp.float32)
    out = jnp.einsum('pitw,ptwj->pitj', window, matrix, precision=HIGH)
    return out.reshape(rows, cols)

def reference(image, keyframe, offsets):
    table = cosine_table()

    def first_pass(section):
        ext = jnp.pad(section.astype(jnp.float32), ((2, 2), (1, 1)))
        center = ext[2:-2, 1:-1]
        g_col = (ext[2:-2, 2:] - ext[2:-2, :-2]) * 0.5
        g_row = (ext[3:-1, 1:-1] - ext[1:-3, 1:-1]) * 0.5
        return (describe(center, table).astype(jnp.bfloat16), describe(g_col, table), describe(g_row, table))
    desc, d_col, d_row = lax.map(first_pass, image)
    keyref = jnp.take(desc, keyframe, axis=0)
    predref = jnp.concatenate([jnp.zeros_like(desc[:1]), desc[:-1]], axis=0)

    def second_pass(items):
        section, own, dc, dr, kref, pref, offs = items
        kc, kr = displacement(own, dc, dr, kref)
        pc, pr = displacement(own, dc, dr, pref)
        u_col = 0.5 * (kc + pc)
        u_row = 0.5 * (kr + pr)
        extended = jnp.pad(section.astype(jnp.float32), ((2, 2), (0, 0)))
        out = warp(extended, u_col, u_row, offs)
        rows, cols = out.shape
        block = out.reshape(rows // 8, 8, cols // 8, 8).sum(axis=(1, 3))
        return (out.astype(jnp.bfloat16), jnp.stack([u_col, u_row]), block)
    warped, field, block = lax.map(second_pass, (image, desc, d_col, d_row, keyref, predref, offsets))
    total = jnp.cumsum(block, axis=0)
    earlier = jnp.concatenate([jnp.zeros((WIN,) + block.shape[1:], jnp.float32), total[:-WIN]], axis=0)
    pyramid = (total - earlier) / 512.0
    return (warped, field, pyramid)
```

```python
import functools

import jax
import jax.numpy as jnp
import ml_dtypes
import numpy as np
from jax import lax
from jax.experimental import pallas as pl
from jax.experimental.pallas import tpu as pltpu
from jax.sharding import PartitionSpec as P

PATCH = 64
KCOEF = 8
WIN = 8
REG = 4.0
BOX = 8
LANES = 128
PAD = 16
MESH = pl.DeviceIdType.MESH
F32 = jnp.float32
BF16 = jnp.bfloat16


def np_split(value, terms):
    parts = []
    rest = np.asarray(value, np.float64)
    for _ in range(terms):
        part = rest.astype(np.float32).astype(ml_dtypes.bfloat16)
        parts.append(part)
        rest = rest - part.astype(np.float64)
    return parts


def tables(rows):
    index = np.arange(PATCH, dtype=np.float64)
    order = np.arange(KCOEF, dtype=np.float64)
    table = np.sqrt(2.0 / PATCH) * np.cos(np.pi * (index[None, :] + 0.5) * order[:, None] / PATCH)
    table = table * np.where(order == 0, np.sqrt(0.5), 1.0)[:, None]
    table = table.astype(np.float32).astype(np.float64)
    zero = np.zeros((KCOEF, rows), ml_dtypes.bfloat16)
    first = np.concatenate(np_split(table, 3) + [zero], axis=0)
    ext = rows + 2 * PAD
    slope = np.zeros((KCOEF, ext))
    slope[:, PAD + 1 : PAD + 1 + rows] += 0.5 * table
    slope[:, PAD - 1 : PAD - 1 + rows] -= 0.5 * table
    second = np_split(slope, 3) + [np.zeros((KCOEF, ext), ml_dtypes.bfloat16)]
    for k in range(-1, 3):
        sums = np.zeros((rows // BOX, ext))
        for r in range(rows):
            sums[r // BOX, PAD + r + k] = 1.0
        second.append(sums.astype(ml_dtypes.bfloat16))
    second = np.concatenate(second, axis=0)
    column = np.stack([np.tile(part.T, (1, LANES // KCOEF)) for part in np_split(table, 3)])
    return first, second, column


def split(value, terms):
    parts = []
    for _ in range(terms):
        part = value.astype(BF16)
        parts.append(part)
        value = value - part.astype(F32)
    return parts


def dot(a, b):
    return jnp.dot(a, b, preferred_element_type=F32)


def to_groups(value, width):
    count = value.shape[1] // width
    return jnp.concatenate([value[:, g * width : (g + 1) * width] for g in range(count)], axis=0)


def from_groups(value, count):
    rows = value.shape[0] // count
    return jnp.concatenate([value[g * rows : (g + 1) * rows] for g in range(count)], axis=1)


def taps(shift):
    return (
        -shift * (shift - 1.0) * (shift - 2.0) * (1.0 / 6.0),
        (shift + 1.0) * (shift - 1.0) * (shift - 2.0) * 0.5,
        -(shift + 1.0) * shift * (shift - 2.0) * 0.5,
        (shift + 1.0) * shift * (shift - 1.0) * (1.0 / 6.0),
    )


def stacked(value, times):
    return value if times == 1 else jnp.concatenate([value] * times, axis=0)


def kernel(
    n, tiles, kf_ref, off_ref, first_ref, second_ref, column_ref, x_hbm,
    out_hbm, field_ref, pyr_ref,
    xext, coldct, expand, pool, compact, comm, shifted, vert, weights, normal, obuf, brecv, bsend, wsum,
    load_sem, store_sem, halo_ssem, halo_rsem, ssem, rsem, bssem, brsem,
):
    me = lax.axis_index("sec")
    mt = lax.axis_index("tile")
    rows, cols = obuf.shape
    group = LANES // KCOEF * PATCH
    groups = cols // group
    blocks = cols // LANES
    sums = rows // BOX

    load = pltpu.make_async_copy(x_hbm.at[0], xext.at[pl.ds(PAD, rows)], load_sem)
    load.start()

    barrier = pltpu.get_barrier_semaphore()

    def greet(q, carry):
        pl.semaphore_signal(barrier, inc=1, device_id={"sec": q}, device_id_type=MESH)
        return carry

    lax.fori_loop(0, me, greet, 0)

    @pl.when(mt > 0)
    def _():
        pl.semaphore_signal(barrier, inc=1, device_id={"tile": mt - 1}, device_id_type=MESH)

    @pl.when(mt < tiles - 1)
    def _():
        pl.semaphore_signal(barrier, inc=1, device_id={"tile": mt + 1}, device_id_type=MESH)

    lane = lax.broadcasted_iota(jnp.int32, (PATCH, LANES), 1)
    for term in range(3):
        base = column_ref[term].astype(F32)
        for p in range(group // PATCH):
            coldct[term, p * PATCH : (p + 1) * PATCH, :] = jnp.where(
                lane // KCOEF == p, base, 0.0
            ).astype(BF16)

    load.wait()

    def first_dct(g):
        part = dot(first_ref[...], xext[PAD : PAD + rows, g * group : (g + 1) * group])
        return part[0:KCOEF] + part[KCOEF : 2 * KCOEF] + part[2 * KCOEF : 3 * KCOEF]

    t_rows = [first_dct(g) for g in range(groups)]
    t_group = jnp.concatenate(t_rows, axis=0)
    parts = split(t_group, 2)
    size = t_group.shape[0]
    wide = dot(jnp.concatenate(parts, axis=0), coldct[0])
    desc = from_groups(wide[:size] + wide[size:] + dot(parts[0], coldct[1]), groups).astype(BF16)
    comm[me] = desc

    pl.semaphore_wait(
        barrier,
        (n - 1 - me) + (mt > 0).astype(jnp.int32) + (mt < tiles - 1).astype(jnp.int32),
    )

    def desc_copy(target):
        return pltpu.make_async_remote_copy(
            src_ref=comm.at[me], dst_ref=comm.at[me], send_sem=ssem.at[target], recv_sem=rsem.at[me],
            device_id={"sec": target}, device_id_type=MESH,
        )

    def send_desc(step, carry):
        desc_copy(n - 1 - step).start()
        return carry

    lax.fori_loop(0, n - 1 - me, send_desc, 0)

    to_next = pltpu.make_async_remote_copy(
        src_ref=x_hbm.at[0, pl.ds(rows - PAD, PAD)], dst_ref=xext.at[pl.ds(0, PAD)],
        send_sem=halo_ssem.at[0], recv_sem=halo_rsem.at[0],
        device_id={"tile": jnp.minimum(mt + 1, tiles - 1)}, device_id_type=MESH,
    )
    to_last = pltpu.make_async_remote_copy(
        src_ref=x_hbm.at[0, pl.ds(0, PAD)], dst_ref=xext.at[pl.ds(PAD + rows, PAD)],
        send_sem=halo_ssem.at[1], recv_sem=halo_rsem.at[1],
        device_id={"tile": jnp.maximum(mt - 1, 0)}, device_id_type=MESH,
    )

    @pl.when(mt < tiles - 1)
    def _():
        to_next.start()

    @pl.when(mt > 0)
    def _():
        to_last.start()

    @pl.when(mt == 0)
    def _():
        xext[0:PAD, :] = jnp.zeros((PAD, cols), BF16)

    @pl.when(mt == tiles - 1)
    def _():
        xext[PAD + rows : 2 * PAD + rows, :] = jnp.zeros((PAD, cols), BF16)

    row_of = lax.broadcasted_iota(jnp.int32, (LANES, group), 0)
    col_of = lax.broadcasted_iota(jnp.int32, (LANES, group), 1)
    expand[...] = jnp.where(row_of // KCOEF == col_of // PATCH, 1.0, 0.0).astype(BF16)
    row_of = lax.broadcasted_iota(jnp.int32, (group, LANES), 0)
    col_of = lax.broadcasted_iota(jnp.int32, (group, LANES), 1)
    pool[...] = jnp.where(row_of // BOX == col_of, 1.0, 0.0).astype(BF16)
    row_of = lax.broadcasted_iota(jnp.int32, compact.shape, 0)
    col_of = lax.broadcasted_iota(jnp.int32, compact.shape, 1)
    compact[...] = jnp.where(row_of // KCOEF == col_of, 1.0, 0.0).astype(BF16)
    zeros = jnp.zeros((vert.shape[0], LANES), F32)
    vert[:, 0:LANES] = zeros
    vert[:, LANES + cols : 2 * LANES + cols] = zeros

    t_full = jnp.concatenate(t_rows, axis=1)
    where = lax.broadcasted_iota(jnp.int32, (KCOEF, cols), 1)
    after = jnp.where(where == cols - 1, 0.0, pltpu.roll(t_full, cols - 1, 1))
    before = jnp.where(where == 0, 0.0, pltpu.roll(t_full, 1, 1))
    tx_group = to_groups((after - before) * 0.5, group)

    @pl.when(mt < tiles - 1)
    def _():
        to_last.wait_recv()

    @pl.when(mt > 0)
    def _():
        to_next.wait_recv()

    ty_rows = []
    for g in range(groups):
        part = dot(second_ref[...], xext[:, g * group : (g + 1) * group])
        ty_rows.append(part[0:KCOEF] + part[KCOEF : 2 * KCOEF] + part[2 * KCOEF : 3 * KCOEF])
        for k in range(4):
            at = 4 * KCOEF + k * sums
            shifted[k, 0:sums, g * group : (g + 1) * group] = part[at : at + sums]
    ty_group = jnp.concatenate(ty_rows, axis=0)

    both = jnp.concatenate([tx_group, ty_group], axis=0)
    parts = split(both, 3)
    size = both.shape[0]
    wide = dot(jnp.concatenate(parts, axis=0), coldct[0])
    mid = dot(jnp.concatenate(parts[:2], axis=0), coldct[1])
    slopes = wide[:size] + (wide[size : 2 * size] + mid[:size]) + (
        wide[2 * size :] + mid[size:] + dot(parts[0], coldct[2])
    )
    half = size // 2
    dx = from_groups(slopes[:half], groups)
    dy = from_groups(slopes[half:], groups)

    def row_total(value):
        for step in (4, 2, 1):
            value = value + pltpu.roll(value, step, 0)
        return value

    def spread(values):
        lhs = jnp.concatenate([to_groups(v, LANES) for v in values], axis=0)
        size = lhs.shape[0]
        wide = dot(jnp.concatenate(split(lhs, 3), axis=0), expand[...])
        total = wide[:size] + (wide[size : 2 * size] + wide[2 * size :])
        step = size // len(values)
        return [from_groups(total[i * step : (i + 1) * step], groups) for i in range(len(values))]

    def narrow(values):
        lhs = jnp.concatenate(values, axis=0)
        size = lhs.shape[0]
        wide = dot(jnp.concatenate(split(lhs, 3), axis=0), compact[...])
        total = wide[:size] + (wide[size : 2 * size] + wide[2 * size :])
        step = size // len(values)
        return [total[i * step : (i + 1) * step] for i in range(len(values))]

    normals = [row_total(dx * dx), row_total(dx * dy), row_total(dy * dy)]
    gxx, gxy, gyy = spread(normals)
    gxx = gxx + REG
    gyy = gyy + REG
    normal[0] = gxx
    normal[1] = gxy
    normal[2] = gyy
    normal[3] = 1.0 / (gxx * gyy - gxy * gxy)

    def prepare(v, carry):
        at = pl.ds(pl.multiple_of(v * LANES, LANES), LANES)
        block = xext[:, at].astype(F32)
        height = block.shape[0]
        for k in range(4):
            moved = block if k == 1 else pltpu.roll(block, (height - (k - 1)) % height, 0)
            shifted[k, sums : sums + rows, at] = moved[PAD : PAD + rows]
        return carry

    lax.fori_loop(0, blocks, prepare, 0)

    def wait_desc(q, carry):
        pltpu.make_async_remote_copy(
            src_ref=comm.at[q], dst_ref=comm.at[q], send_sem=ssem.at[q], recv_sem=rsem.at[q],
            device_id={"sec": q}, device_id_type=MESH,
        ).wait_recv()
        return carry

    lax.fori_loop(0, me, wait_desc, 0)

    keyref = comm[kf_ref[0]].astype(F32)
    predref = jnp.where(me > 0, comm[jnp.maximum(me - 1, 0)].astype(F32), 0.0)
    diff = 0.5 * (keyref + predref) - desc.astype(F32)
    slants = [row_total(dx * diff), row_total(dy * diff)]
    bx, by = spread(slants)
    ux = (normal[2] * bx - normal[1] * by) * normal[3]
    uy = (normal[0] * by - normal[1] * bx) * normal[3]
    for k, weight in enumerate(taps(ux)):
        weights[k] = weight
    for k, weight in enumerate(taps(uy)):
        weights[4 + k] = weight

    lane8 = lax.broadcasted_iota(jnp.int32, (BOX, LANES), 1)

    def vertical(low, count):
        times = count // BOX

        def run(v, carry):
            at = pl.ds(pl.multiple_of(v * LANES, LANES), LANES)
            total = stacked(weights[4, :, at], times) * shifted[0, low : low + count, at]
            for k in range(1, 4):
                total = total + stacked(weights[4 + k, :, at], times) * shifted[k, low : low + count, at]
            vert[low : low + count, pl.ds(pl.multiple_of((v + 1) * LANES, LANES), LANES)] = total
            return carry

        return run

    def horizontal(low, count, store):
        times = count // BOX

        def run(v, carry):
            span = slice(low, low + count)
            left = vert[span, pl.ds(pl.multiple_of(v * LANES, LANES), LANES)]
            center = vert[span, pl.ds(pl.multiple_of((v + 1) * LANES, LANES), LANES)]
            right = vert[span, pl.ds(pl.multiple_of((v + 2) * LANES, LANES), LANES)]
            lanes = stacked(lane8, times)
            even = jnp.where(lanes >= 96, left, center)
            odd = jnp.where(lanes < 32, right, center)
            even = pltpu.roll(even, (LANES - off_ref[0, 2 * v]) % LANES, 1)
            odd = pltpu.roll(odd, (LANES - off_ref[0, 2 * v + 1]) % LANES, 1)
            at = pl.ds(pl.multiple_of(v * LANES, LANES), LANES)
            total = None
            for k in range(-1, 3):
                mine = ((lanes - k + LANES) % LANES) < PATCH
                both = jnp.where(mine, even, odd)
                if k != 0:
                    both = pltpu.roll(both, (LANES - k) % LANES, 1)
                term = stacked(weights[k + 1, :, at], times) * both
                total = term if total is None else total + term
            store(at, total)
            return carry

        return run

    def store_sums(at, value):
        wsum[:, at] = value

    def store_rows(at, value):
        obuf[:, at] = value.astype(BF16)

    lax.fori_loop(0, blocks, vertical(0, sums), 0, unroll=4)
    lax.fori_loop(0, blocks, horizontal(0, sums, store_sums), 0, unroll=4)
    lhs = to_groups(wsum[...], group)
    size = lhs.shape[0]
    wide = dot(jnp.concatenate(split(lhs, 3), axis=0), pool[...])
    block = from_groups(wide[:size] + (wide[size : 2 * size] + wide[2 * size :]), groups)
    bsend[...] = block

    def block_copy(d):
        return pltpu.make_async_remote_copy(
            src_ref=bsend, dst_ref=brecv.at[d - 1], send_sem=bssem.at[d - 1], recv_sem=brsem.at[d - 1],
            device_id={"sec": jnp.minimum(me + d, n - 1)}, device_id_type=MESH,
        )

    reach = min(WIN, n)
    for d in range(reach - 1, 0, -1):
        @pl.when(me + d < n)
        def _():
            block_copy(d).start()

    lax.fori_loop(0, blocks, vertical(sums, rows), 0)
    lax.fori_loop(0, blocks, horizontal(sums, rows, store_rows), 0)
    store = pltpu.make_async_copy(obuf, out_hbm.at[0], store_sem)
    store.start()

    gxx, gxy, gyy, bx, by = narrow(normals + slants)
    gxx = gxx + REG
    gyy = gyy + REG
    det = gxx * gyy - gxy * gxy
    ux = (gyy * bx - gxy * by) / det
    uy = (gxx * by - gxy * bx) / det
    field_ref[0, 0] = ux[0:1]
    field_ref[0, 1] = uy[0:1]

    pyr_ref[0] = block
    for d in range(1, reach):
        @pl.when(me >= d)
        def _():
            block_copy(d).wait_recv()
            pyr_ref[0] = pyr_ref[0] + brecv[d - 1]
    pyr_ref[0] = pyr_ref[0] * (1.0 / (BOX * BOX * WIN))

    def sent_desc(step, carry):
        desc_copy(n - 1 - step).wait_send()
        return carry

    lax.fori_loop(0, n - 1 - me, sent_desc, 0)
    for d in range(reach - 1, 0, -1):
        @pl.when(me + d < n)
        def _():
            block_copy(d).wait_send()

    @pl.when(mt < tiles - 1)
    def _():
        to_next.wait_send()

    @pl.when(mt > 0)
    def _():
        to_last.wait_send()

    store.wait()


def body(n, tiles, image, keyframe, offsets):
    _, rows, cols = image.shape
    first, second, column = tables(rows)
    ext = rows + 2 * PAD
    sums = rows // BOX
    coefs = cols // PATCH * KCOEF
    group = LANES // KCOEF * PATCH
    smem = pl.BlockSpec(memory_space=pltpu.SMEM)
    vmem = pl.BlockSpec(memory_space=pltpu.VMEM)
    hbm = pl.BlockSpec(memory_space=pl.ANY)
    dma = pltpu.SemaphoreType.DMA
    return pl.pallas_call(
        functools.partial(kernel, n, tiles),
        out_shape=(
            jax.ShapeDtypeStruct(image.shape, BF16),
            jax.ShapeDtypeStruct((1, 2, 1, cols // PATCH), F32),
            jax.ShapeDtypeStruct((1, sums, cols // BOX), F32),
        ),
        in_specs=[smem, smem, vmem, vmem, vmem, hbm],
        out_specs=(hbm, vmem, vmem),
        scratch_shapes=[
            pltpu.VMEM((ext, cols), BF16),
            pltpu.VMEM((3, group, LANES), BF16),
            pltpu.VMEM((LANES, group), BF16),
            pltpu.VMEM((group, LANES), BF16),
            pltpu.VMEM((coefs, cols // PATCH), BF16),
            pltpu.VMEM((n, KCOEF, coefs), BF16),
            pltpu.VMEM((4, sums + rows, cols), F32),
            pltpu.VMEM((sums + rows, cols + 2 * LANES), F32),
            pltpu.VMEM((8, KCOEF, cols), F32),
            pltpu.VMEM((4, KCOEF, cols), F32),
            pltpu.VMEM((rows, cols), BF16),
            pltpu.VMEM((WIN - 1, sums, cols // BOX), F32),
            pltpu.VMEM((sums, cols // BOX), F32),
            pltpu.VMEM((sums, cols), F32),
            dma,
            dma,
            dma((2,)),
            dma((2,)),
            dma((n,)),
            dma((n,)),
            dma((WIN - 1,)),
            dma((WIN - 1,)),
        ],
        compiler_params=pltpu.CompilerParams(collective_id=0, has_side_effects=True),
    )(keyframe, offsets, jnp.asarray(first), jnp.asarray(second), jnp.asarray(column), image)


def solution(mesh):
    return jax.shard_map(
        functools.partial(body, mesh.shape["sec"], mesh.shape["tile"]),
        mesh=mesh,
        in_specs=(P(("slab", "sec"), "tile", None), P(("slab", "sec")), P(("slab", "sec"), None)),
        out_specs=(
            P(("slab", "sec"), "tile", None),
            P(("slab", "sec"), None, "tile", None),
            P(("slab", "sec"), "tile", None),
        ),
        check_vma=False,
    )
```

```python
import functools

import jax
import jax.numpy as jnp
import ml_dtypes
import numpy as np
from jax import lax
from jax.experimental import pallas as pl
from jax.experimental.pallas import tpu as pltpu
from jax.sharding import PartitionSpec as P

PATCH = 64
KCOEF = 8
WIN = 8
REG = 4.0
BOX = 8
LANES = 128
PAD = 16
MESH = pl.DeviceIdType.MESH
F32 = jnp.float32
BF16 = jnp.bfloat16


def np_split(value, terms):
    parts = []
    rest = np.asarray(value, np.float64)
    for _ in range(terms):
        part = rest.astype(np.float32).astype(ml_dtypes.bfloat16)
        parts.append(part)
        rest = rest - part.astype(np.float64)
    return parts


def tables(rows):
    index = np.arange(PATCH, dtype=np.float64)
    order = np.arange(KCOEF, dtype=np.float64)
    table = np.sqrt(2.0 / PATCH) * np.cos(np.pi * (index[None, :] + 0.5) * order[:, None] / PATCH)
    table = table * np.where(order == 0, np.sqrt(0.5), 1.0)[:, None]
    table = table.astype(np.float32).astype(np.float64)
    zero = np.zeros((KCOEF, rows), ml_dtypes.bfloat16)
    first = np.concatenate(np_split(table, 3) + [zero], axis=0)
    ext = rows + 2 * PAD
    slope = np.zeros((KCOEF, ext))
    slope[:, PAD + 1 : PAD + 1 + rows] += 0.5 * table
    slope[:, PAD - 1 : PAD - 1 + rows] -= 0.5 * table
    second = np_split(slope, 3) + [np.zeros((KCOEF, ext), ml_dtypes.bfloat16)]
    for k in range(-1, 3):
        sums = np.zeros((rows // BOX, ext))
        for r in range(rows):
            sums[r // BOX, PAD + r + k] = 1.0
        second.append(sums.astype(ml_dtypes.bfloat16))
    second = np.concatenate(second, axis=0)
    column = np.stack([np.tile(part.T, (1, LANES // KCOEF)) for part in np_split(table, 3)])
    return first, second, column


def split(value, terms):
    parts = []
    for _ in range(terms):
        part = value.astype(BF16)
        parts.append(part)
        value = value - part.astype(F32)
    return parts


def dot(a, b):
    return jnp.dot(a, b, preferred_element_type=F32)


def to_groups(value, width):
    count = value.shape[1] // width
    return jnp.concatenate([value[:, g * width : (g + 1) * width] for g in range(count)], axis=0)


def from_groups(value, count):
    rows = value.shape[0] // count
    return jnp.concatenate([value[g * rows : (g + 1) * rows] for g in range(count)], axis=1)


def taps(shift):
    return (
        -shift * (shift - 1.0) * (shift - 2.0) * (1.0 / 6.0),
        (shift + 1.0) * (shift - 1.0) * (shift - 2.0) * 0.5,
        -(shift + 1.0) * shift * (shift - 2.0) * 0.5,
        (shift + 1.0) * shift * (shift - 1.0) * (1.0 / 6.0),
    )


def stacked(value, times):
    return value if times == 1 else jnp.concatenate([value] * times, axis=0)


def kernel(
    n, tiles, kf_hbm, off_hbm, first_hbm, second_hbm, column_hbm, x_hbm,
    obuf, field_ref, pyr_ref,
    kf_ref, off_ref, first_ref, second_ref, column_ref, xext, coldct, expand, pool, compact, comm, shifted, vert, weights, normal, brecv, bsend, wsum,
    load_sem, table_sem, halo_ssem, halo_rsem, ssem, rsem, bssem, brsem,
):
    me = lax.axis_index("sec")
    mt = lax.axis_index("tile")
    _, rows, cols = obuf.shape
    group = LANES // KCOEF * PATCH
    groups = cols // group
    blocks = cols // LANES
    sums = rows // BOX

    barrier = pltpu.get_barrier_semaphore()
    load = pltpu.make_async_copy(x_hbm.at[0], xext.at[pl.ds(PAD, rows)], load_sem)
    fetches = [
        pltpu.make_async_copy(source, target, table_sem.at[i])
        for i, (source, target) in enumerate((
            (column_hbm, column_ref), (first_hbm, first_ref), (second_hbm, second_ref),
            (kf_hbm, kf_ref), (off_hbm, off_ref),
        ))
    ]
    fetches[0].start()
    fetches[1].start()
    load.start()
    for fetch in fetches[2:]:
        fetch.start()

    def greet(q, carry):
        pl.semaphore_signal(barrier, inc=1, device_id={"sec": q}, device_id_type=MESH)
        return carry

    lax.fori_loop(0, me, greet, 0)

    @pl.when(mt > 0)
    def _():
        pl.semaphore_signal(barrier, inc=1, device_id={"tile": mt - 1}, device_id_type=MESH)

    @pl.when(mt < tiles - 1)
    def _():
        pl.semaphore_signal(barrier, inc=1, device_id={"tile": mt + 1}, device_id_type=MESH)

    fetches[0].wait()
    lane = lax.broadcasted_iota(jnp.int32, (PATCH, LANES), 1)
    for term in range(3):
        base = column_ref[term].astype(F32)
        for p in range(group // PATCH):
            coldct[term, p * PATCH : (p + 1) * PATCH, :] = jnp.where(
                lane // KCOEF == p, base, 0.0
            ).astype(BF16)

    fetches[1].wait()
    load.wait()

    def first_dct(g):
        part = dot(first_ref[...], xext[PAD : PAD + rows, g * group : (g + 1) * group])
        return part[0:KCOEF] + part[KCOEF : 2 * KCOEF] + part[2 * KCOEF : 3 * KCOEF]

    t_rows = [first_dct(g) for g in range(groups)]
    t_group = jnp.concatenate(t_rows, axis=0)
    parts = split(t_group, 2)
    size = t_group.shape[0]
    wide = dot(jnp.concatenate(parts, axis=0), coldct[0])
    desc = from_groups(wide[:size] + wide[size:] + dot(parts[0], coldct[1]), groups).astype(BF16)
    comm[me] = desc

    pl.semaphore_wait(
        barrier,
        (n - 1 - me) + (mt > 0).astype(jnp.int32) + (mt < tiles - 1).astype(jnp.int32),
    )

    def desc_copy(target):
        return pltpu.make_async_remote_copy(
            src_ref=comm.at[me], dst_ref=comm.at[me], send_sem=ssem.at[target], recv_sem=rsem.at[me],
            device_id={"sec": target}, device_id_type=MESH,
        )

    def send_desc(step, carry):
        desc_copy(n - 1 - step).start()
        return carry

    lax.fori_loop(0, n - 1 - me, send_desc, 0)

    to_next = pltpu.make_async_remote_copy(
        src_ref=x_hbm.at[0, pl.ds(rows - PAD, PAD)], dst_ref=xext.at[pl.ds(0, PAD)],
        send_sem=halo_ssem.at[0], recv_sem=halo_rsem.at[0],
        device_id={"tile": jnp.minimum(mt + 1, tiles - 1)}, device_id_type=MESH,
    )
    to_last = pltpu.make_async_remote_copy(
        src_ref=x_hbm.at[0, pl.ds(0, PAD)], dst_ref=xext.at[pl.ds(PAD + rows, PAD)],
        send_sem=halo_ssem.at[1], recv_sem=halo_rsem.at[1],
        device_id={"tile": jnp.maximum(mt - 1, 0)}, device_id_type=MESH,
    )

    @pl.when(mt < tiles - 1)
    def _():
        to_next.start()

    @pl.when(mt > 0)
    def _():
        to_last.start()

    @pl.when(mt == 0)
    def _():
        xext[0:PAD, :] = jnp.zeros((PAD, cols), BF16)

    @pl.when(mt == tiles - 1)
    def _():
        xext[PAD + rows : 2 * PAD + rows, :] = jnp.zeros((PAD, cols), BF16)

    row_of = lax.broadcasted_iota(jnp.int32, (LANES, group), 0)
    col_of = lax.broadcasted_iota(jnp.int32, (LANES, group), 1)
    expand[...] = jnp.where(row_of // KCOEF == col_of // PATCH, 1.0, 0.0).astype(BF16)
    row_of = lax.broadcasted_iota(jnp.int32, (group, LANES), 0)
    col_of = lax.broadcasted_iota(jnp.int32, (group, LANES), 1)
    pool[...] = jnp.where(row_of // BOX == col_of, 1.0, 0.0).astype(BF16)
    row_of = lax.broadcasted_iota(jnp.int32, compact.shape, 0)
    col_of = lax.broadcasted_iota(jnp.int32, compact.shape, 1)
    compact[...] = jnp.where(row_of // KCOEF == col_of, 1.0, 0.0).astype(BF16)
    zeros = jnp.zeros((vert.shape[0], LANES), F32)
    vert[:, 0:LANES] = zeros
    vert[:, LANES + cols : 2 * LANES + cols] = zeros

    t_full = jnp.concatenate(t_rows, axis=1)
    where = lax.broadcasted_iota(jnp.int32, (KCOEF, cols), 1)
    after = jnp.where(where == cols - 1, 0.0, pltpu.roll(t_full, cols - 1, 1))
    before = jnp.where(where == 0, 0.0, pltpu.roll(t_full, 1, 1))
    tx_group = to_groups((after - before) * 0.5, group)

    @pl.when(mt < tiles - 1)
    def _():
        to_last.wait_recv()

    @pl.when(mt > 0)
    def _():
        to_next.wait_recv()

    fetches[2].wait()
    ty_rows = []
    for g in range(groups):
        part = dot(second_ref[...], xext[:, g * group : (g + 1) * group])
        ty_rows.append(part[0:KCOEF] + part[KCOEF : 2 * KCOEF] + part[2 * KCOEF : 3 * KCOEF])
        for k in range(4):
            at = 4 * KCOEF + k * sums
            shifted[k, 0:sums, g * group : (g + 1) * group] = part[at : at + sums]
    ty_group = jnp.concatenate(ty_rows, axis=0)

    both = jnp.concatenate([tx_group, ty_group], axis=0)
    parts = split(both, 3)
    size = both.shape[0]
    wide = dot(jnp.concatenate(parts, axis=0), coldct[0])
    mid = dot(jnp.concatenate(parts[:2], axis=0), coldct[1])
    slopes = wide[:size] + (wide[size : 2 * size] + mid[:size]) + (
        wide[2 * size :] + mid[size:] + dot(parts[0], coldct[2])
    )
    half = size // 2
    dx = from_groups(slopes[:half], groups)
    dy = from_groups(slopes[half:], groups)

    def row_total(value):
        for step in (4, 2, 1):
            value = value + pltpu.roll(value, step, 0)
        return value

    def spread(values):
        lhs = jnp.concatenate([to_groups(v, LANES) for v in values], axis=0)
        size = lhs.shape[0]
        wide = dot(jnp.concatenate(split(lhs, 3), axis=0), expand[...])
        total = wide[:size] + (wide[size : 2 * size] + wide[2 * size :])
        step = size // len(values)
        return [from_groups(total[i * step : (i + 1) * step], groups) for i in range(len(values))]

    def narrow(values):
        lhs = jnp.concatenate(values, axis=0)
        size = lhs.shape[0]
        wide = dot(jnp.concatenate(split(lhs, 3), axis=0), compact[...])
        total = wide[:size] + (wide[size : 2 * size] + wide[2 * size :])
        step = size // len(values)
        return [total[i * step : (i + 1) * step] for i in range(len(values))]

    normals = [row_total(dx * dx), row_total(dx * dy), row_total(dy * dy)]
    gxx, gxy, gyy = spread(normals)
    gxx = gxx + REG
    gyy = gyy + REG
    normal[0] = gxx
    normal[1] = gxy
    normal[2] = gyy
    normal[3] = 1.0 / (gxx * gyy - gxy * gxy)

    def prepare(v, carry):
        at = pl.ds(pl.multiple_of(v * LANES, LANES), LANES)
        block = xext[:, at].astype(F32)
        height = block.shape[0]
        for k in range(4):
            moved = block if k == 1 else pltpu.roll(block, (height - (k - 1)) % height, 0)
            shifted[k, sums : sums + rows, at] = moved[PAD : PAD + rows]
        return carry

    @pl.when(me >= n // 2)
    def _():
        lax.fori_loop(0, blocks, prepare, 0, unroll=4)

    fetches[3].wait()
    fetches[4].wait()

    def wait_desc(q, carry):
        pltpu.make_async_remote_copy(
            src_ref=comm.at[q], dst_ref=comm.at[q], send_sem=ssem.at[q], recv_sem=rsem.at[q],
            device_id={"sec": q}, device_id_type=MESH,
        ).wait_recv()
        return carry

    lax.fori_loop(0, me, wait_desc, 0)

    keyref = comm[kf_ref[0]].astype(F32)
    predref = jnp.where(me > 0, comm[jnp.maximum(me - 1, 0)].astype(F32), 0.0)
    diff = 0.5 * (keyref + predref) - desc.astype(F32)
    slants = [row_total(dx * diff), row_total(dy * diff)]
    bx, by = spread(slants)
    ux = (normal[2] * bx - normal[1] * by) * normal[3]
    uy = (normal[0] * by - normal[1] * bx) * normal[3]
    for k, weight in enumerate(taps(ux)):
        weights[k] = weight
    for k, weight in enumerate(taps(uy)):
        weights[4 + k] = weight

    lane8 = lax.broadcasted_iota(jnp.int32, (BOX, LANES), 1)

    def vertical(low, count):
        times = count // BOX

        def run(v, carry):
            at = pl.ds(pl.multiple_of(v * LANES, LANES), LANES)
            total = stacked(weights[4, :, at], times) * shifted[0, low : low + count, at]
            for k in range(1, 4):
                total = total + stacked(weights[4 + k, :, at], times) * shifted[k, low : low + count, at]
            vert[low : low + count, pl.ds(pl.multiple_of((v + 1) * LANES, LANES), LANES)] = total
            return carry

        return run

    def horizontal(low, count, store):
        times = count // BOX

        def run(v, carry):
            span = slice(low, low + count)
            left = vert[span, pl.ds(pl.multiple_of(v * LANES, LANES), LANES)]
            center = vert[span, pl.ds(pl.multiple_of((v + 1) * LANES, LANES), LANES)]
            right = vert[span, pl.ds(pl.multiple_of((v + 2) * LANES, LANES), LANES)]
            lanes = stacked(lane8, times)
            even = jnp.where(lanes >= 96, left, center)
            odd = jnp.where(lanes < 32, right, center)
            even = pltpu.roll(even, (LANES - off_ref[0, 2 * v]) % LANES, 1)
            odd = pltpu.roll(odd, (LANES - off_ref[0, 2 * v + 1]) % LANES, 1)
            at = pl.ds(pl.multiple_of(v * LANES, LANES), LANES)
            total = None
            for k in range(-1, 3):
                mine = ((lanes - k + LANES) % LANES) < PATCH
                both = jnp.where(mine, even, odd)
                if k != 0:
                    both = pltpu.roll(both, (LANES - k) % LANES, 1)
                term = stacked(weights[k + 1, :, at], times) * both
                total = term if total is None else total + term
            store(at, total)
            return carry

        return run

    def store_sums(at, value):
        wsum[:, at] = value

    def store_rows(at, value):
        obuf[0, :, at] = value.astype(BF16)

    lax.fori_loop(0, blocks, vertical(0, sums), 0, unroll=16)
    lax.fori_loop(0, blocks, horizontal(0, sums, store_sums), 0, unroll=16)
    lhs = to_groups(wsum[...], group)
    size = lhs.shape[0]
    wide = dot(jnp.concatenate(split(lhs, 3), axis=0), pool[...])
    block = from_groups(wide[:size] + (wide[size : 2 * size] + wide[2 * size :]), groups)
    bsend[...] = block

    def block_copy(d):
        return pltpu.make_async_remote_copy(
            src_ref=bsend, dst_ref=brecv.at[d - 1], send_sem=bssem.at[d - 1], recv_sem=brsem.at[d - 1],
            device_id={"sec": jnp.minimum(me + d, n - 1)}, device_id_type=MESH,
        )

    reach = min(WIN, n)
    for d in range(reach - 1, 0, -1):
        @pl.when(me + d < n)
        def _():
            block_copy(d).start()

    @pl.when(me < n // 2)
    def _():
        lax.fori_loop(0, blocks, prepare, 0, unroll=4)

    lax.fori_loop(0, blocks, vertical(sums, rows), 0, unroll=2)
    lax.fori_loop(0, blocks, horizontal(sums, rows, store_rows), 0, unroll=4)

    gxx, gxy, gyy, bx, by = narrow(normals + slants)
    gxx = gxx + REG
    gyy = gyy + REG
    det = gxx * gyy - gxy * gxy
    ux = (gyy * bx - gxy * by) / det
    uy = (gxx * by - gxy * bx) / det
    field_ref[0, 0] = ux[0:1]
    field_ref[0, 1] = uy[0:1]

    pyr_ref[0] = block
    for d in range(1, reach):
        @pl.when(me >= d)
        def _():
            block_copy(d).wait_recv()
            pyr_ref[0] = pyr_ref[0] + brecv[d - 1]
    pyr_ref[0] = pyr_ref[0] * (1.0 / (BOX * BOX * WIN))

    def sent_desc(step, carry):
        desc_copy(n - 1 - step).wait_send()
        return carry

    lax.fori_loop(0, n - 1 - me, sent_desc, 0)
    for d in range(reach - 1, 0, -1):
        @pl.when(me + d < n)
        def _():
            block_copy(d).wait_send()

    @pl.when(mt < tiles - 1)
    def _():
        to_next.wait_send()

    @pl.when(mt > 0)
    def _():
        to_last.wait_send()


def body(n, tiles, image, keyframe, offsets):
    _, rows, cols = image.shape
    first, second, column = tables(rows)
    ext = rows + 2 * PAD
    sums = rows // BOX
    coefs = cols // PATCH * KCOEF
    group = LANES // KCOEF * PATCH
    vmem = pl.BlockSpec(memory_space=pltpu.VMEM)
    hbm = pl.BlockSpec(memory_space=pltpu.HBM)
    dma = pltpu.SemaphoreType.DMA
    return pl.pallas_call(
        functools.partial(kernel, n, tiles),
        out_shape=(
            pltpu.VMEM(image.shape, BF16),
            pltpu.VMEM((1, 2, 1, cols // PATCH), F32),
            pltpu.VMEM((1, sums, cols // BOX), F32),
        ),
        in_specs=[hbm] * 6,
        out_specs=(vmem, vmem, vmem),
        scratch_shapes=[
            pltpu.SMEM((1,), jnp.int32),
            pltpu.SMEM((1, cols // PATCH), jnp.int32),
            pltpu.VMEM(first.shape, BF16),
            pltpu.VMEM(second.shape, BF16),
            pltpu.VMEM(column.shape, BF16),
            pltpu.VMEM((ext, cols), BF16),
            pltpu.VMEM((3, group, LANES), BF16),
            pltpu.VMEM((LANES, group), BF16),
            pltpu.VMEM((group, LANES), BF16),
            pltpu.VMEM((coefs, cols // PATCH), BF16),
            pltpu.VMEM((n, KCOEF, coefs), BF16),
            pltpu.VMEM((4, sums + rows, cols), F32),
            pltpu.VMEM((sums + rows, cols + 2 * LANES), F32),
            pltpu.VMEM((8, KCOEF, cols), F32),
            pltpu.VMEM((4, KCOEF, cols), F32),
            pltpu.VMEM((WIN - 1, sums, cols // BOX), F32),
            pltpu.VMEM((sums, cols // BOX), F32),
            pltpu.VMEM((sums, cols), F32),
            dma,
            dma((5,)),
            dma((2,)),
            dma((2,)),
            dma((n,)),
            dma((n,)),
            dma((WIN - 1,)),
            dma((WIN - 1,)),
        ],
        compiler_params=pltpu.CompilerParams(collective_id=0, has_side_effects=True),
    )(keyframe, offsets, jnp.asarray(first), jnp.asarray(second), jnp.asarray(column), image)


def solution(mesh):
    return jax.shard_map(
        functools.partial(body, mesh.shape["sec"], mesh.shape["tile"]),
        mesh=mesh,
        in_specs=(P(("slab", "sec"), "tile", None), P(("slab", "sec")), P(("slab", "sec"), None)),
        out_specs=(
            P(("slab", "sec"), "tile", None),
            P(("slab", "sec"), None, "tile", None),
            P(("slab", "sec"), "tile", None),
        ),
        check_vma=False,
    )
```

```python
import functools

import jax
import jax.numpy as jnp
import ml_dtypes
import numpy as np
from jax import lax
from jax.experimental import pallas as pl
from jax.experimental.pallas import tpu as pltpu
from jax.sharding import PartitionSpec as P

PATCH = 64
KCOEF = 8
WIN = 8
REG = 4.0
BOX = 8
LANES = 128
PAD = 16
MESH = pl.DeviceIdType.MESH
F32 = jnp.float32
BF16 = jnp.bfloat16


def np_split(value, terms):
    parts = []
    rest = np.asarray(value, np.float64)
    for _ in range(terms):
        part = rest.astype(np.float32).astype(ml_dtypes.bfloat16)
        parts.append(part)
        rest = rest - part.astype(np.float64)
    return parts


def tables(rows):
    index = np.arange(PATCH, dtype=np.float64)
    order = np.arange(KCOEF, dtype=np.float64)
    table = np.sqrt(2.0 / PATCH) * np.cos(np.pi * (index[None, :] + 0.5) * order[:, None] / PATCH)
    table = table * np.where(order == 0, np.sqrt(0.5), 1.0)[:, None]
    table = table.astype(np.float32).astype(np.float64)
    zero = np.zeros((KCOEF, rows), ml_dtypes.bfloat16)
    first = np.concatenate(np_split(table, 3) + [zero], axis=0)
    ext = rows + 2 * PAD
    slope = np.zeros((KCOEF, ext))
    slope[:, PAD + 1 : PAD + 1 + rows] += 0.5 * table
    slope[:, PAD - 1 : PAD - 1 + rows] -= 0.5 * table
    second = np_split(slope, 3) + [np.zeros((KCOEF, ext), ml_dtypes.bfloat16)]
    for k in range(-1, 3):
        sums = np.zeros((rows // BOX, ext))
        for r in range(rows):
            sums[r // BOX, PAD + r + k] = 1.0
        second.append(sums.astype(ml_dtypes.bfloat16))
    second = np.concatenate(second, axis=0)
    column = np.stack([np.tile(part.T, (1, LANES // KCOEF)) for part in np_split(table, 3)])
    return first, second, column


def split(value, terms):
    parts = []
    for _ in range(terms):
        part = value.astype(BF16)
        parts.append(part)
        value = value - part.astype(F32)
    return parts


def dot(a, b):
    return jnp.dot(a, b, preferred_element_type=F32)


def to_groups(value, width):
    count = value.shape[1] // width
    return jnp.concatenate([value[:, g * width : (g + 1) * width] for g in range(count)], axis=0)


def from_groups(value, count):
    rows = value.shape[0] // count
    return jnp.concatenate([value[g * rows : (g + 1) * rows] for g in range(count)], axis=1)


def taps(shift):
    return (
        -shift * (shift - 1.0) * (shift - 2.0) * (1.0 / 6.0),
        (shift + 1.0) * (shift - 1.0) * (shift - 2.0) * 0.5,
        -(shift + 1.0) * shift * (shift - 2.0) * 0.5,
        (shift + 1.0) * shift * (shift - 1.0) * (1.0 / 6.0),
    )


def kernel(
    n, tiles, kf_hbm, off_hbm, first_hbm, second_hbm, column_hbm, x_hbm,
    obuf, field_ref, pyr_ref,
    kf_ref, off_ref, first_ref, second_ref, column_ref, xext, coldct, expand, pool, compact, comm, shifted, weights, normal, brecv, bsend, wsum,
    load_sem, table_sem, halo_ssem, halo_rsem, ssem, rsem, bssem, brsem,
):
    me = lax.axis_index("sec")
    mt = lax.axis_index("tile")
    _, rows, cols = obuf.shape
    group = LANES // KCOEF * PATCH
    groups = cols // group
    blocks = cols // LANES
    sums = rows // BOX

    barrier = pltpu.get_barrier_semaphore()
    loads = [
        pltpu.make_async_copy(
            x_hbm.at[0, :, pl.ds(g * group, group)],
            xext.at[pl.ds(PAD, rows), pl.ds(g * group, group)],
            load_sem.at[g],
        )
        for g in range(groups)
    ]
    fetches = [
        pltpu.make_async_copy(source, target, table_sem.at[i])
        for i, (source, target) in enumerate((
            (column_hbm, column_ref), (first_hbm, first_ref), (second_hbm, second_ref),
            (kf_hbm, kf_ref), (off_hbm, off_ref),
        ))
    ]
    fetches[0].start()
    fetches[1].start()
    for load in loads:
        load.start()
    for fetch in fetches[2:]:
        fetch.start()

    def greet(q, carry):
        pl.semaphore_signal(barrier, inc=1, device_id={"sec": q}, device_id_type=MESH)
        return carry

    lax.fori_loop(0, me, greet, 0)

    @pl.when(mt > 0)
    def _():
        pl.semaphore_signal(barrier, inc=1, device_id={"tile": mt - 1}, device_id_type=MESH)

    @pl.when(mt < tiles - 1)
    def _():
        pl.semaphore_signal(barrier, inc=1, device_id={"tile": mt + 1}, device_id_type=MESH)

    fetches[0].wait()
    lane = lax.broadcasted_iota(jnp.int32, (PATCH, LANES), 1)
    for term in range(3):
        base = column_ref[term].astype(F32)
        for p in range(group // PATCH):
            coldct[term, p * PATCH : (p + 1) * PATCH, :] = jnp.where(
                lane // KCOEF == p, base, 0.0
            ).astype(BF16)

    row_of = lax.broadcasted_iota(jnp.int32, (LANES, group), 0)
    col_of = lax.broadcasted_iota(jnp.int32, (LANES, group), 1)
    expand[...] = jnp.where(row_of // KCOEF == col_of // PATCH, 1.0, 0.0).astype(BF16)
    row_of = lax.broadcasted_iota(jnp.int32, (group, LANES), 0)
    col_of = lax.broadcasted_iota(jnp.int32, (group, LANES), 1)
    pool[...] = jnp.where(row_of // BOX == col_of, 1.0, 0.0).astype(BF16)
    row_of = lax.broadcasted_iota(jnp.int32, compact.shape, 0)
    col_of = lax.broadcasted_iota(jnp.int32, compact.shape, 1)
    compact[...] = jnp.where(row_of // KCOEF == col_of, 1.0, 0.0).astype(BF16)
    fetches[1].wait()

    def first_dct(g):
        loads[g].wait()
        part = dot(first_ref[...], xext[PAD : PAD + rows, g * group : (g + 1) * group])
        return part[0:KCOEF] + part[KCOEF : 2 * KCOEF] + part[2 * KCOEF : 3 * KCOEF]

    t_rows = [first_dct(g) for g in range(groups)]
    t_group = jnp.concatenate(t_rows, axis=0)
    parts = split(t_group, 2)
    size = t_group.shape[0]
    wide = dot(jnp.concatenate(parts, axis=0), coldct[0])
    desc = from_groups(wide[:size] + wide[size:] + dot(parts[0], coldct[1]), groups).astype(BF16)
    comm[me] = desc

    pl.semaphore_wait(
        barrier,
        (n - 1 - me) + (mt > 0).astype(jnp.int32) + (mt < tiles - 1).astype(jnp.int32),
    )

    def desc_copy(target):
        return pltpu.make_async_remote_copy(
            src_ref=comm.at[me], dst_ref=comm.at[me], send_sem=ssem.at[target], recv_sem=rsem.at[me],
            device_id={"sec": target}, device_id_type=MESH,
        )

    def send_desc(step, carry):
        desc_copy(n - 1 - step).start()
        return carry

    lax.fori_loop(0, n - 1 - me, send_desc, 0)

    to_next = pltpu.make_async_remote_copy(
        src_ref=x_hbm.at[0, pl.ds(rows - PAD, PAD)], dst_ref=xext.at[pl.ds(0, PAD)],
        send_sem=halo_ssem.at[0], recv_sem=halo_rsem.at[0],
        device_id={"tile": jnp.minimum(mt + 1, tiles - 1)}, device_id_type=MESH,
    )
    to_last = pltpu.make_async_remote_copy(
        src_ref=x_hbm.at[0, pl.ds(0, PAD)], dst_ref=xext.at[pl.ds(PAD + rows, PAD)],
        send_sem=halo_ssem.at[1], recv_sem=halo_rsem.at[1],
        device_id={"tile": jnp.maximum(mt - 1, 0)}, device_id_type=MESH,
    )

    @pl.when(mt < tiles - 1)
    def _():
        to_next.start()

    @pl.when(mt > 0)
    def _():
        to_last.start()

    @pl.when(mt == 0)
    def _():
        xext[0:PAD, :] = jnp.zeros((PAD, cols), BF16)

    @pl.when(mt == tiles - 1)
    def _():
        xext[PAD + rows : 2 * PAD + rows, :] = jnp.zeros((PAD, cols), BF16)

    t_full = jnp.concatenate(t_rows, axis=1)
    where = lax.broadcasted_iota(jnp.int32, (KCOEF, cols), 1)
    after = jnp.where(where == cols - 1, 0.0, pltpu.roll(t_full, cols - 1, 1))
    before = jnp.where(where == 0, 0.0, pltpu.roll(t_full, 1, 1))
    tx_group = to_groups((after - before) * 0.5, group)

    def slope_of(value):
        parts = split(value, 3)
        size = value.shape[0]
        wide = dot(jnp.concatenate(parts, axis=0), coldct[0])
        mid = dot(jnp.concatenate(parts[:2], axis=0), coldct[1])
        total = wide[:size] + (wide[size : 2 * size] + mid[:size]) + (
            wide[2 * size :] + mid[size:] + dot(parts[0], coldct[2])
        )
        return from_groups(total, groups)

    dx = slope_of(tx_group)

    @pl.when(mt < tiles - 1)
    def _():
        to_last.wait_recv()

    @pl.when(mt > 0)
    def _():
        to_next.wait_recv()

    fetches[2].wait()
    ty_rows = []
    for g in range(groups):
        part = dot(second_ref[...], xext[:, g * group : (g + 1) * group])
        ty_rows.append(part[0:KCOEF] + part[KCOEF : 2 * KCOEF] + part[2 * KCOEF : 3 * KCOEF])
        for k in range(4):
            at = 4 * KCOEF + k * sums
            shifted[k, 0:sums, g * group : (g + 1) * group] = part[at : at + sums]
    ty_group = jnp.concatenate(ty_rows, axis=0)

    dy = slope_of(ty_group)

    def row_total(value):
        for step in (4, 2, 1):
            value = value + pltpu.roll(value, step, 0)
        return value

    def spread(values):
        lhs = jnp.concatenate([to_groups(v, LANES) for v in values], axis=0)
        size = lhs.shape[0]
        wide = dot(jnp.concatenate(split(lhs, 3), axis=0), expand[...])
        total = wide[:size] + (wide[size : 2 * size] + wide[2 * size :])
        step = size // len(values)
        return [from_groups(total[i * step : (i + 1) * step], groups) for i in range(len(values))]

    def narrow(values):
        lhs = jnp.concatenate(values, axis=0)
        size = lhs.shape[0]
        wide = dot(jnp.concatenate(split(lhs, 3), axis=0), compact[...])
        total = wide[:size] + (wide[size : 2 * size] + wide[2 * size :])
        step = size // len(values)
        return [total[i * step : (i + 1) * step] for i in range(len(values))]

    normals = [row_total(dx * dx), row_total(dx * dy), row_total(dy * dy)]
    gxx, gxy, gyy = spread(normals)
    gxx = gxx + REG
    gyy = gyy + REG
    normal[0] = gxx
    normal[1] = gxy
    normal[2] = gyy
    normal[3] = 1.0 / (gxx * gyy - gxy * gxy)

    def prepare(v, carry):
        at = pl.ds(pl.multiple_of(v * LANES, LANES), LANES)
        block = xext[:, at].astype(F32)
        height = block.shape[0]
        for k in range(4):
            moved = block if k == 1 else pltpu.roll(block, (height - (k - 1)) % height, 0)
            shifted[k, sums : sums + rows, at] = moved[PAD : PAD + rows]
        return carry

    @pl.when(me >= n // 2)
    def _():
        lax.fori_loop(0, blocks, prepare, 0, unroll=4)

    fetches[3].wait()
    fetches[4].wait()

    def wait_desc(q, carry):
        pltpu.make_async_remote_copy(
            src_ref=comm.at[q], dst_ref=comm.at[q], send_sem=ssem.at[q], recv_sem=rsem.at[q],
            device_id={"sec": q}, device_id_type=MESH,
        ).wait_recv()
        return carry

    lax.fori_loop(0, me, wait_desc, 0)

    keyref = comm[kf_ref[0]].astype(F32)
    predref = jnp.where(me > 0, comm[jnp.maximum(me - 1, 0)].astype(F32), 0.0)
    diff = 0.5 * (keyref + predref) - desc.astype(F32)
    slants = [row_total(dx * diff), row_total(dy * diff)]
    bx, by = spread(slants)
    ux = (normal[2] * bx - normal[1] * by) * normal[3]
    uy = (normal[0] * by - normal[1] * bx) * normal[3]
    for k, weight in enumerate(taps(ux)):
        weights[k] = weight
    for k, weight in enumerate(taps(uy)):
        weights[4 + k] = weight

    lane8 = lax.broadcasted_iota(jnp.int32, (BOX, LANES), 1)
    takes = [((lane8 - k) & (LANES - 1)) < PATCH for k in range(-1, 3)]
    from_left = lane8 >= 96
    from_right = lane8 < 32

    def vertical(v, low, count):
        at = slice(v * LANES, (v + 1) * LANES)
        gains = [weights[4 + k, :, at] for k in range(4)]
        strips = []
        for r in range(low, low + count, BOX):
            total = gains[0] * shifted[0, r : r + BOX, at]
            for k in range(1, 4):
                total = total + gains[k] * shifted[k, r : r + BOX, at]
            strips.append(total)
        return strips

    def horizontal(v, left, center, right, store):
        at = slice(v * LANES, (v + 1) * LANES)
        turn_even = (LANES - off_ref[0, 2 * v]) & (LANES - 1)
        turn_odd = (LANES - off_ref[0, 2 * v + 1]) & (LANES - 1)
        gains = [weights[k, :, at] for k in range(4)]
        for r in range(len(center)):
            even = pltpu.roll(jnp.where(from_left, left[r], center[r]), turn_even, 1)
            odd = pltpu.roll(jnp.where(from_right, right[r], center[r]), turn_odd, 1)
            total = None
            for k in range(-1, 3):
                both = jnp.where(takes[k + 1], even, odd)
                if k != 0:
                    both = pltpu.roll(both, (LANES - k) % LANES, 1)
                term = gains[k + 1] * both
                total = term if total is None else total + term
            store(r * BOX, at, total)

    def warp(low, count, store):
        blank = [jnp.zeros((BOX, LANES), F32)] * (count // BOX)
        left, center = blank, vertical(0, low, count)
        for v in range(blocks):
            right = vertical(v + 1, low, count) if v + 1 < blocks else blank
            horizontal(v, left, center, right, store)
            left, center = center, right

    def store_sums(r, at, value):
        wsum[r : r + BOX, at] = value

    def store_rows(r, at, value):
        obuf[0, r : r + BOX, at] = value.astype(BF16)

    warp(0, sums, store_sums)
    lhs = to_groups(wsum[...], group)
    size = lhs.shape[0]
    wide = dot(jnp.concatenate(split(lhs, 3), axis=0), pool[...])
    block = from_groups(wide[:size] + (wide[size : 2 * size] + wide[2 * size :]), groups)
    bsend[...] = block

    def block_copy(d):
        return pltpu.make_async_remote_copy(
            src_ref=bsend, dst_ref=brecv.at[d - 1], send_sem=bssem.at[d - 1], recv_sem=brsem.at[d - 1],
            device_id={"sec": jnp.minimum(me + d, n - 1)}, device_id_type=MESH,
        )

    reach = min(WIN, n)
    for d in range(reach - 1, 0, -1):
        @pl.when(me + d < n)
        def _():
            block_copy(d).start()

    @pl.when(me < n // 2)
    def _():
        lax.fori_loop(0, blocks, prepare, 0, unroll=4)

    warp(sums, rows, store_rows)

    gxx, gxy, gyy, bx, by = narrow(normals + slants)
    gxx = gxx + REG
    gyy = gyy + REG
    det = gxx * gyy - gxy * gxy
    ux = (gyy * bx - gxy * by) / det
    uy = (gxx * by - gxy * bx) / det
    field_ref[0, 0] = ux[0:1]
    field_ref[0, 1] = uy[0:1]

    pyr_ref[0] = block
    for d in range(1, reach):
        @pl.when(me >= d)
        def _():
            block_copy(d).wait_recv()
            pyr_ref[0] = pyr_ref[0] + brecv[d - 1]
    pyr_ref[0] = pyr_ref[0] * (1.0 / (BOX * BOX * WIN))

    def sent_desc(step, carry):
        desc_copy(n - 1 - step).wait_send()
        return carry

    lax.fori_loop(0, n - 1 - me, sent_desc, 0)
    for d in range(reach - 1, 0, -1):
        @pl.when(me + d < n)
        def _():
            block_copy(d).wait_send()

    @pl.when(mt < tiles - 1)
    def _():
        to_next.wait_send()

    @pl.when(mt > 0)
    def _():
        to_last.wait_send()


def write_out(a, b, c, a_out, b_out, c_out, sem):
    copies = [
        pltpu.make_async_copy(source, target, sem.at[i])
        for i, (source, target) in enumerate(((a, a_out), (b, b_out), (c, c_out)))
    ]
    for copy in copies:
        copy.start()
    for copy in copies:
        copy.wait()


def body(n, tiles, image, keyframe, offsets):
    _, rows, cols = image.shape
    first, second, column = tables(rows)
    ext = rows + 2 * PAD
    sums = rows // BOX
    coefs = cols // PATCH * KCOEF
    group = LANES // KCOEF * PATCH
    vmem = pl.BlockSpec(memory_space=pltpu.VMEM)
    hbm = pl.BlockSpec(memory_space=pltpu.HBM)
    dma = pltpu.SemaphoreType.DMA
    results = pl.pallas_call(
        functools.partial(kernel, n, tiles),
        out_shape=(
            pltpu.VMEM(image.shape, BF16),
            pltpu.VMEM((1, 2, 1, cols // PATCH), F32),
            pltpu.VMEM((1, sums, cols // BOX), F32),
        ),
        in_specs=[hbm] * 6,
        out_specs=(vmem, vmem, vmem),
        scratch_shapes=[
            pltpu.SMEM((1,), jnp.int32),
            pltpu.SMEM((1, cols // PATCH), jnp.int32),
            pltpu.VMEM(first.shape, BF16),
            pltpu.VMEM(second.shape, BF16),
            pltpu.VMEM(column.shape, BF16),
            pltpu.VMEM((ext, cols), BF16),
            pltpu.VMEM((3, group, LANES), BF16),
            pltpu.VMEM((LANES, group), BF16),
            pltpu.VMEM((group, LANES), BF16),
            pltpu.VMEM((coefs, cols // PATCH), BF16),
            pltpu.VMEM((n, KCOEF, coefs), BF16),
            pltpu.VMEM((4, sums + rows, cols), F32),
            pltpu.VMEM((8, KCOEF, cols), F32),
            pltpu.VMEM((4, KCOEF, cols), F32),
            pltpu.VMEM((WIN - 1, sums, cols // BOX), F32),
            pltpu.VMEM((sums, cols // BOX), F32),
            pltpu.VMEM((sums, cols), F32),
            dma((cols // group,)),
            dma((5,)),
            dma((2,)),
            dma((2,)),
            dma((n,)),
            dma((n,)),
            dma((WIN - 1,)),
            dma((WIN - 1,)),
        ],
        compiler_params=pltpu.CompilerParams(collective_id=0, has_side_effects=True),
    )(keyframe, offsets, jnp.asarray(first), jnp.asarray(second), jnp.asarray(column), image)
    return pl.pallas_call(
        write_out,
        out_shape=tuple(jax.ShapeDtypeStruct(r.shape, r.dtype) for r in results),
        in_specs=[vmem] * 3,
        out_specs=(hbm,) * 3,
        scratch_shapes=[dma((3,))],
    )(*[pltpu.with_memory_space_constraint(r, pltpu.VMEM) for r in results])


def solution(mesh):
    return jax.shard_map(
        functools.partial(body, mesh.shape["sec"], mesh.shape["tile"]),
        mesh=mesh,
        in_specs=(P(("slab", "sec"), "tile", None), P(("slab", "sec")), P(("slab", "sec"), None)),
        out_specs=(
            P(("slab", "sec"), "tile", None),
            P(("slab", "sec"), None, "tile", None),
            P(("slab", "sec"), "tile", None),
        ),
        check_vma=False,
    )
```

```python
import functools

import jax
import jax.numpy as jnp
import ml_dtypes
import numpy as np
from jax import lax
from jax.experimental import pallas as pl
from jax.experimental.pallas import tpu as pltpu
from jax.sharding import PartitionSpec as P

PATCH = 64
KCOEF = 8
WIN = 8
REG = 4.0
BOX = 8
LANES = 128
PAD = 16
U_PREP, U_VS, U_HS, U_V, U_H = 2, 4, 8, 1, 2
MESH = pl.DeviceIdType.MESH
F32 = jnp.float32
BF16 = jnp.bfloat16


def np_split(value, terms):
    parts = []
    rest = np.asarray(value, np.float64)
    for _ in range(terms):
        part = rest.astype(np.float32).astype(ml_dtypes.bfloat16)
        parts.append(part)
        rest = rest - part.astype(np.float64)
    return parts


def tables(rows):
    index = np.arange(PATCH, dtype=np.float64)
    order = np.arange(KCOEF, dtype=np.float64)
    table = np.sqrt(2.0 / PATCH) * np.cos(np.pi * (index[None, :] + 0.5) * order[:, None] / PATCH)
    table = table * np.where(order == 0, np.sqrt(0.5), 1.0)[:, None]
    table = table.astype(np.float32).astype(np.float64)
    zero = np.zeros((KCOEF, rows), ml_dtypes.bfloat16)
    first = np.concatenate(np_split(table, 3) + [zero], axis=0)
    ext = rows + 2 * PAD
    slope = np.zeros((KCOEF, ext))
    slope[:, PAD + 1 : PAD + 1 + rows] += 0.5 * table
    slope[:, PAD - 1 : PAD - 1 + rows] -= 0.5 * table
    second = np_split(slope, 3) + [np.zeros((KCOEF, ext), ml_dtypes.bfloat16)]
    for k in range(-1, 3):
        sums = np.zeros((rows // BOX, ext))
        for r in range(rows):
            sums[r // BOX, PAD + r + k] = 1.0
        second.append(sums.astype(ml_dtypes.bfloat16))
    second = np.concatenate(second, axis=0)
    column = np.stack([np.tile(part.T, (1, LANES // KCOEF)) for part in np_split(table, 3)])
    return first, second, column


def split(value, terms):
    parts = []
    for _ in range(terms):
        part = value.astype(BF16)
        parts.append(part)
        value = value - part.astype(F32)
    return parts


def dot(a, b):
    return jnp.dot(a, b, preferred_element_type=F32)


def to_groups(value, width):
    count = value.shape[1] // width
    return jnp.concatenate([value[:, g * width : (g + 1) * width] for g in range(count)], axis=0)


def from_groups(value, count):
    rows = value.shape[0] // count
    return jnp.concatenate([value[g * rows : (g + 1) * rows] for g in range(count)], axis=1)


def taps(shift):
    return (
        -shift * (shift - 1.0) * (shift - 2.0) * (1.0 / 6.0),
        (shift + 1.0) * (shift - 1.0) * (shift - 2.0) * 0.5,
        -(shift + 1.0) * shift * (shift - 2.0) * 0.5,
        (shift + 1.0) * shift * (shift - 1.0) * (1.0 / 6.0),
    )


def stacked(value, times):
    return value if times == 1 else jnp.concatenate([value] * times, axis=0)


def kernel(
    n, tiles, kf_hbm, off_hbm, first_hbm, second_hbm, column_hbm, x_hbm,
    obuf, field_ref, pyr_ref,
    kf_ref, off_ref, first_ref, second_ref, column_ref, xext, coldct, expand, pool, compact, comm, shifted, vert, weights, normal, brecv, bsend, wsum, tgroup,
    load_sem, table_sem, halo_ssem, halo_rsem, ssem, rsem, bssem, brsem,
):
    me = lax.axis_index("sec")
    mt = lax.axis_index("tile")
    _, rows, cols = obuf.shape
    group = LANES // KCOEF * PATCH
    groups = cols // group
    blocks = cols // LANES
    sums = rows // BOX

    barrier = pltpu.get_barrier_semaphore()
    load = pltpu.make_async_copy(x_hbm.at[0], xext.at[pl.ds(PAD, rows)], load_sem)
    fetches = [
        pltpu.make_async_copy(source, target, table_sem.at[i])
        for i, (source, target) in enumerate((
            (column_hbm, column_ref), (first_hbm, first_ref), (second_hbm, second_ref),
            (kf_hbm, kf_ref), (off_hbm, off_ref),
        ))
    ]
    fetches[0].start()
    fetches[1].start()
    load.start()
    for fetch in fetches[2:]:
        fetch.start()

    def greet(q, carry):
        pl.semaphore_signal(barrier, inc=1, device_id={"sec": q}, device_id_type=MESH)
        return carry

    lax.fori_loop(0, me, greet, 0)

    @pl.when(mt > 0)
    def _():
        pl.semaphore_signal(barrier, inc=1, device_id={"tile": mt - 1}, device_id_type=MESH)

    @pl.when(mt < tiles - 1)
    def _():
        pl.semaphore_signal(barrier, inc=1, device_id={"tile": mt + 1}, device_id_type=MESH)

    fetches[0].wait()
    lane = lax.broadcasted_iota(jnp.int32, (PATCH, LANES), 1)

    def build_columns(p, carry):
        at = pl.ds(pl.multiple_of(p * PATCH, PATCH), PATCH)
        for term in range(3):
            coldct[term, at, :] = jnp.where(
                lane // KCOEF == p, column_ref[term].astype(F32), 0.0
            ).astype(BF16)
        return carry

    lax.fori_loop(0, group // PATCH, build_columns, 0)

    def build_squares(p, carry):
        at = pl.ds(pl.multiple_of(p * LANES, LANES), LANES)
        row_of = lax.broadcasted_iota(jnp.int32, (LANES, LANES), 0)
        col_of = lax.broadcasted_iota(jnp.int32, (LANES, LANES), 1)
        expand[:, at] = jnp.where(
            row_of // KCOEF == (col_of + p * LANES) // PATCH, 1.0, 0.0
        ).astype(BF16)
        pool[at, :] = jnp.where((row_of + p * LANES) // BOX == col_of, 1.0, 0.0).astype(BF16)
        return carry

    lax.fori_loop(0, group // LANES, build_squares, 0)

    def build_compact(p, carry):
        at = pl.ds(pl.multiple_of(p * LANES, LANES), LANES)
        shape = (LANES, compact.shape[1])
        row_of = lax.broadcasted_iota(jnp.int32, shape, 0) + p * LANES
        col_of = lax.broadcasted_iota(jnp.int32, shape, 1)
        compact[at, :] = jnp.where(row_of // KCOEF == col_of, 1.0, 0.0).astype(BF16)
        return carry

    lax.fori_loop(0, compact.shape[0] // LANES, build_compact, 0)

    def clear(r, carry):
        at = pl.ds(pl.multiple_of(r * BOX, BOX), BOX)
        vert[at, 0:LANES] = jnp.zeros((BOX, LANES), F32)
        vert[at, LANES + cols : 2 * LANES + cols] = jnp.zeros((BOX, LANES), F32)
        return carry

    lax.fori_loop(0, (sums + rows) // BOX, clear, 0)
    fetches[1].wait()
    load.wait()

    def first_dct(g, carry):
        at = pl.ds(pl.multiple_of(g * group, group), group)
        part = dot(first_ref[...], xext[PAD : PAD + rows, at])
        tgroup[0, pl.ds(pl.multiple_of(g * KCOEF, KCOEF), KCOEF), :] = (
            part[0:KCOEF] + part[KCOEF : 2 * KCOEF] + part[2 * KCOEF : 3 * KCOEF]
        )
        return carry

    lax.fori_loop(0, groups, first_dct, 0)
    t_group = tgroup[0]
    parts = split(t_group, 2)
    size = t_group.shape[0]
    wide = dot(jnp.concatenate(parts, axis=0), coldct[0])
    desc = from_groups(wide[:size] + wide[size:] + dot(parts[0], coldct[1]), groups).astype(BF16)
    comm[me] = desc

    pl.semaphore_wait(
        barrier,
        (n - 1 - me) + (mt > 0).astype(jnp.int32) + (mt < tiles - 1).astype(jnp.int32),
    )

    def desc_copy(target):
        return pltpu.make_async_remote_copy(
            src_ref=comm.at[me], dst_ref=comm.at[me], send_sem=ssem.at[target], recv_sem=rsem.at[me],
            device_id={"sec": target}, device_id_type=MESH,
        )

    def send_desc(step, carry):
        desc_copy(n - 1 - step).start()
        return carry

    lax.fori_loop(0, n - 1 - me, send_desc, 0)

    to_next = pltpu.make_async_remote_copy(
        src_ref=x_hbm.at[0, pl.ds(rows - PAD, PAD)], dst_ref=xext.at[pl.ds(0, PAD)],
        send_sem=halo_ssem.at[0], recv_sem=halo_rsem.at[0],
        device_id={"tile": jnp.minimum(mt + 1, tiles - 1)}, device_id_type=MESH,
    )
    to_last = pltpu.make_async_remote_copy(
        src_ref=x_hbm.at[0, pl.ds(0, PAD)], dst_ref=xext.at[pl.ds(PAD + rows, PAD)],
        send_sem=halo_ssem.at[1], recv_sem=halo_rsem.at[1],
        device_id={"tile": jnp.maximum(mt - 1, 0)}, device_id_type=MESH,
    )

    @pl.when(mt < tiles - 1)
    def _():
        to_next.start()

    @pl.when(mt > 0)
    def _():
        to_last.start()

    @pl.when(mt == 0)
    def _():
        def blank(v, carry):
            xext[0:PAD, pl.ds(pl.multiple_of(v * group, group), group)] = jnp.zeros((PAD, group), BF16)
            return carry

        lax.fori_loop(0, groups, blank, 0)

    @pl.when(mt == tiles - 1)
    def _():
        def blank(v, carry):
            at = pl.ds(pl.multiple_of(v * group, group), group)
            xext[PAD + rows : 2 * PAD + rows, at] = jnp.zeros((PAD, group), BF16)
            return carry

        lax.fori_loop(0, groups, blank, 0)

    t_full = from_groups(tgroup[0], groups)
    where = lax.broadcasted_iota(jnp.int32, (KCOEF, cols), 1)
    after = jnp.where(where == cols - 1, 0.0, pltpu.roll(t_full, cols - 1, 1))
    before = jnp.where(where == 0, 0.0, pltpu.roll(t_full, 1, 1))
    tx_group = to_groups((after - before) * 0.5, group)

    @pl.when(mt < tiles - 1)
    def _():
        to_last.wait_recv()

    @pl.when(mt > 0)
    def _():
        to_next.wait_recv()

    fetches[2].wait()
    def second_dct(g, carry):
        at = pl.ds(pl.multiple_of(g * group, group), group)
        part = dot(second_ref[...], xext[:, at])
        tgroup[1, pl.ds(pl.multiple_of(g * KCOEF, KCOEF), KCOEF), :] = (
            part[0:KCOEF] + part[KCOEF : 2 * KCOEF] + part[2 * KCOEF : 3 * KCOEF]
        )
        for k in range(4):
            begin = 4 * KCOEF + k * sums
            shifted[k, 0:sums, at] = part[begin : begin + sums]
        return carry

    lax.fori_loop(0, groups, second_dct, 0)
    ty_group = tgroup[1]
    both = jnp.concatenate([tx_group, ty_group], axis=0)
    parts = split(both, 3)
    size = both.shape[0]
    wide = dot(jnp.concatenate(parts, axis=0), coldct[0])
    mid = dot(jnp.concatenate(parts[:2], axis=0), coldct[1])
    slopes = wide[:size] + (wide[size : 2 * size] + mid[:size]) + (
        wide[2 * size :] + mid[size:] + dot(parts[0], coldct[2])
    )
    half = size // 2
    dx = from_groups(slopes[:half], groups)
    dy = from_groups(slopes[half:], groups)

    def row_total(value):
        for step in (4, 2, 1):
            value = value + pltpu.roll(value, step, 0)
        return value

    def spread(values):
        lhs = jnp.concatenate([to_groups(v, LANES) for v in values], axis=0)
        size = lhs.shape[0]
        wide = dot(jnp.concatenate(split(lhs, 3), axis=0), expand[...])
        total = wide[:size] + (wide[size : 2 * size] + wide[2 * size :])
        step = size // len(values)
        return [from_groups(total[i * step : (i + 1) * step], groups) for i in range(len(values))]

    def narrow(values):
        lhs = jnp.concatenate(values, axis=0)
        size = lhs.shape[0]
        wide = dot(jnp.concatenate(split(lhs, 3), axis=0), compact[...])
        total = wide[:size] + (wide[size : 2 * size] + wide[2 * size :])
        step = size // len(values)
        return [total[i * step : (i + 1) * step] for i in range(len(values))]

    normals = [row_total(dx * dx), row_total(dx * dy), row_total(dy * dy)]
    gxx, gxy, gyy = spread(normals)
    gxx = gxx + REG
    gyy = gyy + REG
    normal[0] = gxx
    normal[1] = gxy
    normal[2] = gyy
    normal[3] = 1.0 / (gxx * gyy - gxy * gxy)

    def prepare(v, carry):
        at = pl.ds(pl.multiple_of(v * LANES, LANES), LANES)
        block = xext[:, at].astype(F32)
        height = block.shape[0]
        for k in range(4):
            moved = block if k == 1 else pltpu.roll(block, (height - (k - 1)) % height, 0)
            shifted[k, sums : sums + rows, at] = moved[PAD : PAD + rows]
        return carry

    @pl.when(me >= n // 2)
    def _():
        lax.fori_loop(0, blocks, prepare, 0, unroll=U_PREP)

    fetches[3].wait()
    fetches[4].wait()

    def wait_desc(q, carry):
        pltpu.make_async_remote_copy(
            src_ref=comm.at[q], dst_ref=comm.at[q], send_sem=ssem.at[q], recv_sem=rsem.at[q],
            device_id={"sec": q}, device_id_type=MESH,
        ).wait_recv()
        return carry

    lax.fori_loop(0, me, wait_desc, 0)

    keyref = comm[kf_ref[0]].astype(F32)
    predref = jnp.where(me > 0, comm[jnp.maximum(me - 1, 0)].astype(F32), 0.0)
    diff = 0.5 * (keyref + predref) - desc.astype(F32)
    slants = [row_total(dx * diff), row_total(dy * diff)]
    bx, by = spread(slants)
    ux = (normal[2] * bx - normal[1] * by) * normal[3]
    uy = (normal[0] * by - normal[1] * bx) * normal[3]
    for k, weight in enumerate(taps(ux)):
        weights[k] = weight
    for k, weight in enumerate(taps(uy)):
        weights[4 + k] = weight

    lane8 = lax.broadcasted_iota(jnp.int32, (BOX, LANES), 1)

    def vertical(low, count):
        times = count // BOX

        def run(v, carry):
            at = pl.ds(pl.multiple_of(v * LANES, LANES), LANES)
            total = stacked(weights[4, :, at], times) * shifted[0, low : low + count, at]
            for k in range(1, 4):
                total = total + stacked(weights[4 + k, :, at], times) * shifted[k, low : low + count, at]
            vert[low : low + count, pl.ds(pl.multiple_of((v + 1) * LANES, LANES), LANES)] = total
            return carry

        return run

    def horizontal(low, count, store):
        times = count // BOX

        def run(v, carry):
            span = slice(low, low + count)
            left = vert[span, pl.ds(pl.multiple_of(v * LANES, LANES), LANES)]
            center = vert[span, pl.ds(pl.multiple_of((v + 1) * LANES, LANES), LANES)]
            right = vert[span, pl.ds(pl.multiple_of((v + 2) * LANES, LANES), LANES)]
            lanes = stacked(lane8, times)
            even = jnp.where(lanes >= 96, left, center)
            odd = jnp.where(lanes < 32, right, center)
            even = pltpu.roll(even, (LANES - off_ref[0, 2 * v]) & (LANES - 1), 1)
            odd = pltpu.roll(odd, (LANES - off_ref[0, 2 * v + 1]) & (LANES - 1), 1)
            at = pl.ds(pl.multiple_of(v * LANES, LANES), LANES)
            total = None
            for k in range(-1, 3):
                mine = ((lanes - k) & (LANES - 1)) < PATCH
                both = jnp.where(mine, even, odd)
                if k != 0:
                    both = pltpu.roll(both, (LANES - k) % LANES, 1)
                term = stacked(weights[k + 1, :, at], times) * both
                total = term if total is None else total + term
            store(at, total)
            return carry

        return run

    def store_sums(at, value):
        wsum[:, at] = value

    def store_rows(at, value):
        obuf[0, :, at] = value.astype(BF16)

    lax.fori_loop(0, blocks, vertical(0, sums), 0, unroll=U_VS)
    lax.fori_loop(0, blocks, horizontal(0, sums, store_sums), 0, unroll=U_HS)
    lhs = to_groups(wsum[...], group)
    size = lhs.shape[0]
    wide = dot(jnp.concatenate(split(lhs, 3), axis=0), pool[...])
    block = from_groups(wide[:size] + (wide[size : 2 * size] + wide[2 * size :]), groups)
    bsend[...] = block

    def block_copy(d):
        return pltpu.make_async_remote_copy(
            src_ref=bsend, dst_ref=brecv.at[d - 1], send_sem=bssem.at[d - 1], recv_sem=brsem.at[d - 1],
            device_id={"sec": jnp.minimum(me + d, n - 1)}, device_id_type=MESH,
        )

    reach = min(WIN, n)
    for d in range(reach - 1, 0, -1):
        @pl.when(me + d < n)
        def _():
            block_copy(d).start()

    @pl.when(me < n // 2)
    def _():
        lax.fori_loop(0, blocks, prepare, 0, unroll=U_PREP)

    lax.fori_loop(0, blocks, vertical(sums, rows), 0, unroll=U_V)
    lax.fori_loop(0, blocks, horizontal(sums, rows, store_rows), 0, unroll=U_H)

    gxx, gxy, gyy, bx, by = narrow(normals + slants)
    gxx = gxx + REG
    gyy = gyy + REG
    det = gxx * gyy - gxy * gxy
    ux = (gyy * bx - gxy * by) / det
    uy = (gxx * by - gxy * bx) / det
    field_ref[0, 0] = ux[0:1]
    field_ref[0, 1] = uy[0:1]

    pyr_ref[0] = block
    for d in range(1, reach):
        @pl.when(me >= d)
        def _():
            block_copy(d).wait_recv()
            pyr_ref[0] = pyr_ref[0] + brecv[d - 1]
    pyr_ref[0] = pyr_ref[0] * (1.0 / (BOX * BOX * WIN))

    def sent_desc(step, carry):
        desc_copy(n - 1 - step).wait_send()
        return carry

    lax.fori_loop(0, n - 1 - me, sent_desc, 0)
    for d in range(reach - 1, 0, -1):
        @pl.when(me + d < n)
        def _():
            block_copy(d).wait_send()

    @pl.when(mt < tiles - 1)
    def _():
        to_next.wait_send()

    @pl.when(mt > 0)
    def _():
        to_last.wait_send()


def write_out(a, b, c, a_out, b_out, c_out, sem):
    copies = [
        pltpu.make_async_copy(source, target, sem.at[i])
        for i, (source, target) in enumerate(((a, a_out), (b, b_out), (c, c_out)))
    ]
    for copy in copies:
        copy.start()
    for copy in copies:
        copy.wait()


def body(n, tiles, image, keyframe, offsets):
    _, rows, cols = image.shape
    first, second, column = tables(rows)
    ext = rows + 2 * PAD
    sums = rows // BOX
    coefs = cols // PATCH * KCOEF
    group = LANES // KCOEF * PATCH
    vmem = pl.BlockSpec(memory_space=pltpu.VMEM)
    hbm = pl.BlockSpec(memory_space=pltpu.HBM)
    dma = pltpu.SemaphoreType.DMA
    results = pl.pallas_call(
        functools.partial(kernel, n, tiles),
        out_shape=(
            pltpu.VMEM(image.shape, BF16),
            pltpu.VMEM((1, 2, 1, cols // PATCH), F32),
            pltpu.VMEM((1, sums, cols // BOX), F32),
        ),
        in_specs=[hbm] * 6,
        out_specs=(vmem, vmem, vmem),
        scratch_shapes=[
            pltpu.SMEM((1,), jnp.int32),
            pltpu.SMEM((1, cols // PATCH), jnp.int32),
            pltpu.VMEM(first.shape, BF16),
            pltpu.VMEM(second.shape, BF16),
            pltpu.VMEM(column.shape, BF16),
            pltpu.VMEM((ext, cols), BF16),
            pltpu.VMEM((3, group, LANES), BF16),
            pltpu.VMEM((LANES, group), BF16),
            pltpu.VMEM((group, LANES), BF16),
            pltpu.VMEM((coefs, cols // PATCH), BF16),
            pltpu.VMEM((n, KCOEF, coefs), BF16),
            pltpu.VMEM((4, sums + rows, cols), F32),
            pltpu.VMEM((sums + rows, cols + 2 * LANES), F32),
            pltpu.VMEM((8, KCOEF, cols), F32),
            pltpu.VMEM((4, KCOEF, cols), F32),
            pltpu.VMEM((WIN - 1, sums, cols // BOX), F32),
            pltpu.VMEM((sums, cols // BOX), F32),
            pltpu.VMEM((sums, cols), F32),
            pltpu.VMEM((2, cols // group * KCOEF, group), F32),
            dma,
            dma((5,)),
            dma((2,)),
            dma((2,)),
            dma((n,)),
            dma((n,)),
            dma((WIN - 1,)),
            dma((WIN - 1,)),
        ],
        compiler_params=pltpu.CompilerParams(collective_id=0, has_side_effects=True),
    )(keyframe, offsets, jnp.asarray(first), jnp.asarray(second), jnp.asarray(column), image)
    return pl.pallas_call(
        write_out,
        out_shape=tuple(jax.ShapeDtypeStruct(r.shape, r.dtype) for r in results),
        in_specs=[vmem] * 3,
        out_specs=(hbm,) * 3,
        scratch_shapes=[dma((3,))],
    )(*[pltpu.with_memory_space_constraint(r, pltpu.VMEM) for r in results])


def solution(mesh):
    return jax.shard_map(
        functools.partial(body, mesh.shape["sec"], mesh.shape["tile"]),
        mesh=mesh,
        in_specs=(P(("slab", "sec"), "tile", None), P(("slab", "sec")), P(("slab", "sec"), None)),
        out_specs=(
            P(("slab", "sec"), "tile", None),
            P(("slab", "sec"), None, "tile", None),
            P(("slab", "sec"), "tile", None),
        ),
        check_vma=False,
    )
```

```python
import functools

import jax
import jax.numpy as jnp
import ml_dtypes
import numpy as np
from jax import lax
from jax.experimental import pallas as pl
from jax.experimental.pallas import tpu as pltpu
from jax.sharding import PartitionSpec as P

PATCH = 64
KCOEF = 8
WIN = 8
REG = 4.0
BOX = 8
LANES = 128
PAD = 16
U_HS, U_H = 32, 4
MESH = pl.DeviceIdType.MESH
F32 = jnp.float32
BF16 = jnp.bfloat16


def np_split(value, terms):
    parts = []
    rest = np.asarray(value, np.float64)
    for _ in range(terms):
        part = rest.astype(np.float32).astype(ml_dtypes.bfloat16)
        parts.append(part)
        rest = rest - part.astype(np.float64)
    return parts


def tables(rows):
    index = np.arange(PATCH, dtype=np.float64)
    order = np.arange(KCOEF, dtype=np.float64)
    table = np.sqrt(2.0 / PATCH) * np.cos(np.pi * (index[None, :] + 0.5) * order[:, None] / PATCH)
    table = table * np.where(order == 0, np.sqrt(0.5), 1.0)[:, None]
    table = table.astype(np.float32).astype(np.float64)
    zero = np.zeros((KCOEF, rows), ml_dtypes.bfloat16)
    first = np.concatenate(np_split(table, 3) + [zero], axis=0)
    ext = rows + 2 * PAD
    slope = np.zeros((KCOEF, ext))
    slope[:, PAD + 1 : PAD + 1 + rows] += 0.5 * table
    slope[:, PAD - 1 : PAD - 1 + rows] -= 0.5 * table
    second = np_split(slope, 3) + [np.zeros((KCOEF, ext), ml_dtypes.bfloat16)]
    for k in range(-1, 3):
        sums = np.zeros((rows // BOX, ext))
        for r in range(rows):
            sums[r // BOX, PAD + r + k] = 1.0
        second.append(sums.astype(ml_dtypes.bfloat16))
    second = np.concatenate(second, axis=0)
    column = np.stack([np.tile(part.T, (1, LANES // KCOEF)) for part in np_split(table, 3)])
    return first, second, column


def split(value, terms):
    parts = []
    for _ in range(terms):
        part = value.astype(BF16)
        parts.append(part)
        value = value - part.astype(F32)
    return parts


def dot(a, b):
    return jnp.dot(a, b, preferred_element_type=F32)


def to_groups(value, width):
    count = value.shape[1] // width
    return jnp.concatenate([value[:, g * width : (g + 1) * width] for g in range(count)], axis=0)


def from_groups(value, count):
    rows = value.shape[0] // count
    return jnp.concatenate([value[g * rows : (g + 1) * rows] for g in range(count)], axis=1)


def taps(shift):
    return (
        -shift * (shift - 1.0) * (shift - 2.0) * (1.0 / 6.0),
        (shift + 1.0) * (shift - 1.0) * (shift - 2.0) * 0.5,
        -(shift + 1.0) * shift * (shift - 2.0) * 0.5,
        (shift + 1.0) * shift * (shift - 1.0) * (1.0 / 6.0),
    )


def stacked(value, times):
    return value if times == 1 else jnp.concatenate([value] * times, axis=0)


def kernel(
    n, tiles, kf_hbm, off_hbm, first_hbm, second_hbm, column_hbm, x_hbm,
    obuf, field_ref, pyr_ref,
    kf_ref, off_ref, first_ref, second_ref, column_ref, xext, coldct, expand, pool, compact, comm, shifted, vert, weights, normal, brecv, bsend, wsum, tgroup,
    load_sem, table_sem, halo_ssem, halo_rsem, ssem, rsem, bssem, brsem,
):
    me = lax.axis_index("sec")
    mt = lax.axis_index("tile")
    _, rows, cols = obuf.shape
    group = LANES // KCOEF * PATCH
    groups = cols // group
    blocks = cols // LANES
    sums = rows // BOX

    barrier = pltpu.get_barrier_semaphore()
    load = pltpu.make_async_copy(x_hbm.at[0], xext.at[pl.ds(PAD, rows)], load_sem)
    fetches = [
        pltpu.make_async_copy(source, target, table_sem.at[i])
        for i, (source, target) in enumerate((
            (column_hbm, column_ref), (first_hbm, first_ref), (second_hbm, second_ref),
            (kf_hbm, kf_ref), (off_hbm, off_ref),
        ))
    ]
    fetches[0].start()
    fetches[1].start()
    load.start()
    for fetch in fetches[2:]:
        fetch.start()

    def greet(q, carry):
        pl.semaphore_signal(barrier, inc=1, device_id={"sec": q}, device_id_type=MESH)
        return carry

    lax.fori_loop(0, me, greet, 0)

    @pl.when(mt > 0)
    def _():
        pl.semaphore_signal(barrier, inc=1, device_id={"tile": mt - 1}, device_id_type=MESH)

    @pl.when(mt < tiles - 1)
    def _():
        pl.semaphore_signal(barrier, inc=1, device_id={"tile": mt + 1}, device_id_type=MESH)

    fetches[0].wait()
    lane = lax.broadcasted_iota(jnp.int32, (PATCH, LANES), 1)

    def build_columns(p, carry):
        at = pl.ds(pl.multiple_of(p * PATCH, PATCH), PATCH)
        for term in range(3):
            coldct[term, at, :] = jnp.where(
                lane // KCOEF == p, column_ref[term].astype(F32), 0.0
            ).astype(BF16)
        return carry

    lax.fori_loop(0, group // PATCH, build_columns, 0)

    def build_squares(p, carry):
        at = pl.ds(pl.multiple_of(p * LANES, LANES), LANES)
        row_of = lax.broadcasted_iota(jnp.int32, (LANES, LANES), 0)
        col_of = lax.broadcasted_iota(jnp.int32, (LANES, LANES), 1)
        expand[:, at] = jnp.where(
            row_of // KCOEF == (col_of + p * LANES) // PATCH, 1.0, 0.0
        ).astype(BF16)
        pool[at, :] = jnp.where((row_of + p * LANES) // BOX == col_of, 1.0, 0.0).astype(BF16)
        return carry

    lax.fori_loop(0, group // LANES, build_squares, 0)

    def build_compact(p, carry):
        at = pl.ds(pl.multiple_of(p * LANES, LANES), LANES)
        shape = (LANES, compact.shape[1])
        row_of = lax.broadcasted_iota(jnp.int32, shape, 0) + p * LANES
        col_of = lax.broadcasted_iota(jnp.int32, shape, 1)
        compact[at, :] = jnp.where(row_of // KCOEF == col_of, 1.0, 0.0).astype(BF16)
        return carry

    lax.fori_loop(0, compact.shape[0] // LANES, build_compact, 0)

    def clear(r, carry):
        at = pl.ds(pl.multiple_of(r * BOX, BOX), BOX)
        vert[at, 0:LANES] = jnp.zeros((BOX, LANES), F32)
        vert[at, LANES + cols : 2 * LANES + cols] = jnp.zeros((BOX, LANES), F32)
        return carry

    lax.fori_loop(0, rows // BOX, clear, 0)
    fetches[1].wait()
    load.wait()

    def first_dct(g, carry):
        at = pl.ds(pl.multiple_of(g * group, group), group)
        part = dot(first_ref[...], xext[PAD : PAD + rows, at])
        tgroup[0, pl.ds(pl.multiple_of(g * KCOEF, KCOEF), KCOEF), :] = (
            part[0:KCOEF] + part[KCOEF : 2 * KCOEF] + part[2 * KCOEF : 3 * KCOEF]
        )
        return carry

    lax.fori_loop(0, groups, first_dct, 0)
    t_group = tgroup[0]
    parts = split(t_group, 2)
    size = t_group.shape[0]
    wide = dot(jnp.concatenate(parts, axis=0), coldct[0])
    desc = from_groups(wide[:size] + wide[size:] + dot(parts[0], coldct[1]), groups).astype(BF16)
    comm[me] = desc

    pl.semaphore_wait(
        barrier,
        (n - 1 - me) + (mt > 0).astype(jnp.int32) + (mt < tiles - 1).astype(jnp.int32),
    )

    def desc_copy(target):
        return pltpu.make_async_remote_copy(
            src_ref=comm.at[me], dst_ref=comm.at[me], send_sem=ssem.at[target], recv_sem=rsem.at[me],
            device_id={"sec": target}, device_id_type=MESH,
        )

    def send_desc(step, carry):
        desc_copy(n - 1 - step).start()
        return carry

    lax.fori_loop(0, n - 1 - me, send_desc, 0)

    to_next = pltpu.make_async_remote_copy(
        src_ref=x_hbm.at[0, pl.ds(rows - PAD, PAD)], dst_ref=xext.at[pl.ds(0, PAD)],
        send_sem=halo_ssem.at[0], recv_sem=halo_rsem.at[0],
        device_id={"tile": jnp.minimum(mt + 1, tiles - 1)}, device_id_type=MESH,
    )
    to_last = pltpu.make_async_remote_copy(
        src_ref=x_hbm.at[0, pl.ds(0, PAD)], dst_ref=xext.at[pl.ds(PAD + rows, PAD)],
        send_sem=halo_ssem.at[1], recv_sem=halo_rsem.at[1],
        device_id={"tile": jnp.maximum(mt - 1, 0)}, device_id_type=MESH,
    )

    @pl.when(mt < tiles - 1)
    def _():
        to_next.start()

    @pl.when(mt > 0)
    def _():
        to_last.start()

    @pl.when(mt == 0)
    def _():
        def blank(v, carry):
            xext[0:PAD, pl.ds(pl.multiple_of(v * group, group), group)] = jnp.zeros((PAD, group), BF16)
            return carry

        lax.fori_loop(0, groups, blank, 0)

    @pl.when(mt == tiles - 1)
    def _():
        def blank(v, carry):
            at = pl.ds(pl.multiple_of(v * group, group), group)
            xext[PAD + rows : 2 * PAD + rows, at] = jnp.zeros((PAD, group), BF16)
            return carry

        lax.fori_loop(0, groups, blank, 0)

    t_full = from_groups(tgroup[0], groups)
    where = lax.broadcasted_iota(jnp.int32, (KCOEF, cols), 1)
    after = jnp.where(where == cols - 1, 0.0, pltpu.roll(t_full, cols - 1, 1))
    before = jnp.where(where == 0, 0.0, pltpu.roll(t_full, 1, 1))
    tx_group = to_groups((after - before) * 0.5, group)

    @pl.when(mt < tiles - 1)
    def _():
        to_last.wait_recv()

    @pl.when(mt > 0)
    def _():
        to_next.wait_recv()

    fetches[2].wait()
    def second_dct(g, carry):
        at = pl.ds(pl.multiple_of(g * group, group), group)
        part = dot(second_ref[...], xext[:, at])
        tgroup[1, pl.ds(pl.multiple_of(g * KCOEF, KCOEF), KCOEF), :] = (
            part[0:KCOEF] + part[KCOEF : 2 * KCOEF] + part[2 * KCOEF : 3 * KCOEF]
        )
        for k in range(4):
            begin = 4 * KCOEF + k * sums
            shifted[k, 0:sums, at] = part[begin : begin + sums]
        return carry

    lax.fori_loop(0, groups, second_dct, 0)
    ty_group = tgroup[1]
    both = jnp.concatenate([tx_group, ty_group], axis=0)
    parts = split(both, 3)
    size = both.shape[0]
    wide = dot(jnp.concatenate(parts, axis=0), coldct[0])
    mid = dot(jnp.concatenate(parts[:2], axis=0), coldct[1])
    slopes = wide[:size] + (wide[size : 2 * size] + mid[:size]) + (
        wide[2 * size :] + mid[size:] + dot(parts[0], coldct[2])
    )
    half = size // 2
    dx = from_groups(slopes[:half], groups)
    dy = from_groups(slopes[half:], groups)

    def row_total(value):
        for step in (4, 2, 1):
            value = value + pltpu.roll(value, step, 0)
        return value

    def spread(values):
        lhs = jnp.concatenate([to_groups(v, LANES) for v in values], axis=0)
        size = lhs.shape[0]
        wide = dot(jnp.concatenate(split(lhs, 3), axis=0), expand[...])
        total = wide[:size] + (wide[size : 2 * size] + wide[2 * size :])
        step = size // len(values)
        return [from_groups(total[i * step : (i + 1) * step], groups) for i in range(len(values))]

    def narrow(values):
        lhs = jnp.concatenate(values, axis=0)
        size = lhs.shape[0]
        wide = dot(jnp.concatenate(split(lhs, 3), axis=0), compact[...])
        total = wide[:size] + (wide[size : 2 * size] + wide[2 * size :])
        step = size // len(values)
        return [total[i * step : (i + 1) * step] for i in range(len(values))]

    normals = [row_total(dx * dx), row_total(dx * dy), row_total(dy * dy)]
    gxx, gxy, gyy = spread(normals)
    gxx = gxx + REG
    gyy = gyy + REG
    normal[0] = gxx
    normal[1] = gxy
    normal[2] = gyy
    normal[3] = 1.0 / (gxx * gyy - gxy * gxy)

    fetches[3].wait()
    fetches[4].wait()

    def wait_desc(q, carry):
        pltpu.make_async_remote_copy(
            src_ref=comm.at[q], dst_ref=comm.at[q], send_sem=ssem.at[q], recv_sem=rsem.at[q],
            device_id={"sec": q}, device_id_type=MESH,
        ).wait_recv()
        return carry

    lax.fori_loop(0, me, wait_desc, 0)

    keyref = comm[kf_ref[0]].astype(F32)
    predref = jnp.where(me > 0, comm[jnp.maximum(me - 1, 0)].astype(F32), 0.0)
    diff = 0.5 * (keyref + predref) - desc.astype(F32)
    slants = [row_total(dx * diff), row_total(dy * diff)]
    bx, by = spread(slants)
    ux = (normal[2] * bx - normal[1] * by) * normal[3]
    uy = (normal[0] * by - normal[1] * bx) * normal[3]
    for k, weight in enumerate(taps(ux)):
        weights[k] = weight
    for k, weight in enumerate(taps(uy)):
        weights[4 + k] = weight

    lane8 = lax.broadcasted_iota(jnp.int32, (BOX, LANES), 1)

    def block_at(v):
        return pl.ds(pl.multiple_of(v * LANES, LANES), LANES)

    def sums_at(at):
        return [shifted[k, :, at] for k in range(4)]

    def rows_at(at):
        whole = xext[:, at].astype(F32)
        height = whole.shape[0]
        return [
            (whole if k == 0 else pltpu.roll(whole, (height - k) % height, 0))[PAD : PAD + rows]
            for k in range(-1, 3)
        ]

    def vertical(count, fetch):
        times = count // BOX

        def run(v, carry):
            at = block_at(jnp.minimum(v, blocks - 1))
            total = None
            for k, part in enumerate(fetch(at)):
                term = stacked(weights[4 + k, :, at], times) * part
                total = term if total is None else total + term
            vert[0:count, block_at(jnp.where(v < blocks, v + 1, blocks + 2))] = total
            return carry

        return run

    def horizontal(count, store):
        times = count // BOX

        def run(v, carry):
            left = vert[0:count, block_at(v)]
            center = vert[0:count, block_at(v + 1)]
            right = vert[0:count, block_at(v + 2)]
            lanes = stacked(lane8, times)
            even = jnp.where(lanes >= 96, left, center)
            odd = jnp.where(lanes < 32, right, center)
            even = pltpu.roll(even, (LANES - off_ref[0, 2 * v]) & (LANES - 1), 1)
            odd = pltpu.roll(odd, (LANES - off_ref[0, 2 * v + 1]) & (LANES - 1), 1)
            at = block_at(v)
            total = None
            for k in range(-1, 3):
                both = jnp.where(((lanes - k) & (LANES - 1)) < PATCH, even, odd)
                if k != 0:
                    both = pltpu.roll(both, (LANES - k) % LANES, 1)
                term = stacked(weights[k + 1, :, at], times) * both
                total = term if total is None else total + term
            store(at, total)
            return carry

        return run

    def warp(count, fetch, store, unroll):
        down = vertical(count, fetch)
        across = horizontal(count, store)

        def run(v, carry):
            across(v, carry)
            return down(v + 2, carry)

        lax.fori_loop(0, 2, down, 0)
        lax.fori_loop(0, blocks, run, 0, unroll=unroll)

    def store_sums(at, value):
        wsum[:, at] = value

    def store_rows(at, value):
        obuf[0, :, at] = value.astype(BF16)

    lax.fori_loop(0, blocks, vertical(sums, sums_at), 0, unroll=8)
    lax.fori_loop(0, blocks, horizontal(sums, store_sums), 0, unroll=U_HS)
    lhs = to_groups(wsum[...], group)
    size = lhs.shape[0]
    wide = dot(jnp.concatenate(split(lhs, 3), axis=0), pool[...])
    block = from_groups(wide[:size] + (wide[size : 2 * size] + wide[2 * size :]), groups)
    bsend[...] = block

    def block_copy(d):
        return pltpu.make_async_remote_copy(
            src_ref=bsend, dst_ref=brecv.at[d - 1], send_sem=bssem.at[d - 1], recv_sem=brsem.at[d - 1],
            device_id={"sec": jnp.minimum(me + d, n - 1)}, device_id_type=MESH,
        )

    reach = min(WIN, n)
    for d in range(reach - 1, 0, -1):
        @pl.when(me + d < n)
        def _():
            block_copy(d).start()

    warp(rows, rows_at, store_rows, U_H)

    gxx, gxy, gyy, bx, by = narrow(normals + slants)
    gxx = gxx + REG
    gyy = gyy + REG
    det = gxx * gyy - gxy * gxy
    ux = (gyy * bx - gxy * by) / det
    uy = (gxx * by - gxy * bx) / det
    field_ref[0, 0] = ux[0:1]
    field_ref[0, 1] = uy[0:1]

    pyr_ref[0] = block
    for d in range(1, reach):
        @pl.when(me >= d)
        def _():
            block_copy(d).wait_recv()
            pyr_ref[0] = pyr_ref[0] + brecv[d - 1]
    pyr_ref[0] = pyr_ref[0] * (1.0 / (BOX * BOX * WIN))

    def sent_desc(step, carry):
        desc_copy(n - 1 - step).wait_send()
        return carry

    lax.fori_loop(0, n - 1 - me, sent_desc, 0)
    for d in range(reach - 1, 0, -1):
        @pl.when(me + d < n)
        def _():
            block_copy(d).wait_send()

    @pl.when(mt < tiles - 1)
    def _():
        to_next.wait_send()

    @pl.when(mt > 0)
    def _():
        to_last.wait_send()


def write_out(a, b, c, a_out, b_out, c_out, sem):
    copies = [
        pltpu.make_async_copy(source, target, sem.at[i])
        for i, (source, target) in enumerate(((a, a_out), (b, b_out), (c, c_out)))
    ]
    for copy in copies:
        copy.start()
    for copy in copies:
        copy.wait()


def body(n, tiles, image, keyframe, offsets):
    _, rows, cols = image.shape
    first, second, column = tables(rows)
    ext = rows + 2 * PAD
    sums = rows // BOX
    coefs = cols // PATCH * KCOEF
    group = LANES // KCOEF * PATCH
    vmem = pl.BlockSpec(memory_space=pltpu.VMEM)
    hbm = pl.BlockSpec(memory_space=pltpu.HBM)
    dma = pltpu.SemaphoreType.DMA
    results = pl.pallas_call(
        functools.partial(kernel, n, tiles),
        out_shape=(
            pltpu.VMEM(image.shape, BF16),
            pltpu.VMEM((1, 2, 1, cols // PATCH), F32),
            pltpu.VMEM((1, sums, cols // BOX), F32),
        ),
        in_specs=[hbm] * 6,
        out_specs=(vmem, vmem, vmem),
        scratch_shapes=[
            pltpu.SMEM((1,), jnp.int32),
            pltpu.SMEM((1, cols // PATCH), jnp.int32),
            pltpu.VMEM(first.shape, BF16),
            pltpu.VMEM(second.shape, BF16),
            pltpu.VMEM(column.shape, BF16),
            pltpu.VMEM((ext, cols), BF16),
            pltpu.VMEM((3, group, LANES), BF16),
            pltpu.VMEM((LANES, group), BF16),
            pltpu.VMEM((group, LANES), BF16),
            pltpu.VMEM((coefs, cols // PATCH), BF16),
            pltpu.VMEM((n, KCOEF, coefs), BF16),
            pltpu.VMEM((4, sums, cols), F32),
            pltpu.VMEM((rows, cols + 3 * LANES), F32),
            pltpu.VMEM((8, KCOEF, cols), F32),
            pltpu.VMEM((4, KCOEF, cols), F32),
            pltpu.VMEM((WIN - 1, sums, cols // BOX), F32),
            pltpu.VMEM((sums, cols // BOX), F32),
            pltpu.VMEM((sums, cols), F32),
            pltpu.VMEM((2, cols // group * KCOEF, group), F32),
            dma,
            dma((5,)),
            dma((2,)),
            dma((2,)),
            dma((n,)),
            dma((n,)),
            dma((WIN - 1,)),
            dma((WIN - 1,)),
        ],
        compiler_params=pltpu.CompilerParams(collective_id=0, has_side_effects=True),
    )(keyframe, offsets, jnp.asarray(first), jnp.asarray(second), jnp.asarray(column), image)
    return pl.pallas_call(
        write_out,
        out_shape=tuple(jax.ShapeDtypeStruct(r.shape, r.dtype) for r in results),
        in_specs=[vmem] * 3,
        out_specs=(hbm,) * 3,
        scratch_shapes=[dma((3,))],
    )(*[pltpu.with_memory_space_constraint(r, pltpu.VMEM) for r in results])


def solution(mesh):
    return jax.shard_map(
        functools.partial(body, mesh.shape["sec"], mesh.shape["tile"]),
        mesh=mesh,
        in_specs=(P(("slab", "sec"), "tile", None), P(("slab", "sec")), P(("slab", "sec"), None)),
        out_specs=(
            P(("slab", "sec"), "tile", None),
            P(("slab", "sec"), None, "tile", None),
            P(("slab", "sec"), "tile", None),
        ),
        check_vma=False,
    )
```
